128 devices in a mesh: grp: 8 (over y, core), hlp: 16 (over z, x).
Axes of the slice: x: 4, y: 4, z: 4, core: 2. Of those that a mesh axis runs over, the one named last changes fastest.
Arguments:
- pivot_inverse: bfloat16 [8, 2048, 2048], P('grp', 'hlp'), may hold values from -1 to 2, as said below
- cross_block: bfloat16 [8, 3584, 2048], P('grp', 'hlp'), may hold values from -0.375 to 0.375
- contrib_block: float32 [8, 3584, 3584], P('grp', 'hlp'), may hold values from -3 to 3, as said below
- pivot_sources: bfloat16 [8, 2048, 512], P('grp', 'hlp'), may hold values from -6 to 6
- contrib_sources: bfloat16 [8, 3584, 512], P('grp', 'hlp'), may hold values from -6 to 6
- ext_map: int32 [8, 3584], P('grp', 'hlp'), may hold values from 0 to 7167, as said below
- parent_front: float32 [7168, 7168], P(('grp', 'hlp')), may hold values from -6 to 6, as said below
- parent_rhs: float32 [7168, 512], P(('grp', 'hlp')), may hold values from -6 to 6
Outputs:
- solved: bfloat16 [8, 2048, 512], P('grp', 'hlp')
- front_out: float32 [7168, 7168], P(('grp', 'hlp'))
- rhs_out: float32 [7168, 512], P(('grp', 'hlp'))
The draws below stay inside these ranges and needn't reach their ends.
Inputs may be any that keep to these rules, and one draw needn't show every extreme that they name: `ext_map`: the 3584 entries of one child are distinct. Within each aligned block of 224 entries of a child, at most 3 entries fall into any one aligned block of 56 parent rows, and exactly 3 fall into some such block. `pivot_inverse`: lower triangular with positive diagonal. `contrib_block`: each child's block is symmetric. `parent_front`: Symmetric.
All inputs are finite; a program needn't handle non-finite values.
Results may differ from the reference program's by a relative error of at most 0.0043.
Values may be sent and summed in bfloat16 or wider, within the bound.
A program may use at most 128 MiB of HBM per device.

```python
import jax
import jax.numpy as jnp
from jax import lax

P_SIZE = 2048
C = 3584
NP = 7168
NSRC = 512
GROUPS = 8
CAP = 3
N_HLP = 16
DEVICES = 128


def draw_pivot_inverse(key, part):
    first_key, second_key = jax.random.split(key)
    rows_at = jnp.arange(P_SIZE)[:, None]
    cols_at = jnp.arange(P_SIZE)[None, :]
    below = (cols_at < rows_at).astype(jnp.float32)
    diagonal = jnp.exp(jax.random.uniform(first_key, (GROUPS, P_SIZE), jnp.float32, jnp.log(0.5), jnp.log(2.0)))
    strict_part = jnp.clip(jax.random.normal(second_key, (GROUPS, P_SIZE, P_SIZE), jnp.float32), -4.0, 4.0) * (0.6 / jnp.sqrt(1.0 * P_SIZE))
    eye_part = (cols_at == rows_at).astype(jnp.float32)
    whole = strict_part * below[None] + eye_part[None] * diagonal[:, :, None]
    return whole.astype(jnp.bfloat16)


def symmetric_noise(key, shape, scale, bound):
    raw = jax.random.normal(key, shape, jnp.float32)
    mirrored = (raw + jnp.swapaxes(raw, -1, -2)) * 0.70710678
    return jnp.clip(mirrored * scale, -bound, bound)


def draw_contrib_block(key, part):
    return symmetric_noise(jax.random.fold_in(key, 11), (GROUPS, C, C), 0.5, 3.0)


def draw_parent_front(key, part):
    return symmetric_noise(jax.random.fold_in(key, 23), (NP, NP), 1.0, 6.0)


def draw_ext_map(key, part):
    owned = NP // DEVICES
    per_source = C // N_HLP
    slot_at = jnp.arange(NP)
    owner_of = slot_at // owned
    within = slot_at % owned
    helper_of = slot_at % N_HLP
    usable_rank = within // N_HLP

    def one_group(group_key):
        perm_key, source_keys = jax.random.split(group_key)
        slot_perm = jax.vmap(lambda one_key: jax.random.permutation(one_key, owned))(jax.random.split(perm_key, DEVICES))
        rows_flat = (jnp.arange(DEVICES)[:, None] * owned + slot_perm).reshape(-1)

        def one_source(helper, source_key):
            first_key, second_key = jax.random.split(source_key)
            usable = (helper_of == helper) & (usable_rank < CAP)
            pick_order = jax.random.permutation(second_key, NP)
            chosen_slot = jnp.argmin(jnp.where(usable, pick_order, pick_order + 2 * NP))
            chosen = chosen_slot // owned
            priority = jax.random.permutation(first_key, NP)
            priority = jnp.where(owner_of == chosen, priority - NP, priority)
            priority = jnp.where(usable, priority, priority + 3 * NP)
            ranking = jnp.argsort(priority)
            return rows_flat[ranking[:per_source]]
        picked = jax.vmap(one_source)(jnp.arange(N_HLP), jax.random.split(source_keys, N_HLP))
        return picked.reshape(C)
    return jax.vmap(one_group)(jax.random.split(key, GROUPS)).astype(jnp.int32)


def level_of(own_key, shape, cuts, low, largest):
    def one(axis_at, parts):
        steps = jax.random.uniform(jax.random.fold_in(jax.random.fold_in(own_key, 6), axis_at), (parts,), jnp.float32, low / len(cuts), largest / len(cuts))
        return jnp.repeat(jnp.exp(steps), shape[axis_at] // parts).reshape((-1,) + (1,) * (len(shape) - axis_at - 1))

    loudness = one(*cuts[0])
    for cut in cuts[1:]:
        loudness = loudness * one(*cut)
    return loudness


def gaussian(own_key, extent, deviation, limit, shards=(), kind=jnp.bfloat16):
    factor_of = level_of(own_key, extent, shards, -0.22, 0.18) if shards else 1.0
    values = jax.random.normal(own_key, extent, jnp.float32) * deviation * factor_of
    return jnp.minimum(jnp.maximum(values, -limit), limit).astype(kind)


def setup_inputs(seed: int = 0) -> dict:
    seeds = jax.random.split(jax.random.key(seed), 9)
    return {
        "pivot_inverse": draw_pivot_inverse(jax.random.fold_in(seeds[8], 71), 0),
        "cross_block": gaussian(seeds[1], (GROUPS, C, P_SIZE), (P_SIZE // 8) ** -0.5, 0.375, ((0, 8), (1, 16))),
        "contrib_block": draw_contrib_block(jax.random.fold_in(seeds[8], 71), 0),
        "pivot_sources": gaussian(seeds[3], (GROUPS, P_SIZE, NSRC), 1.0, 6.0, ((0, 8), (1, 16))),
        "contrib_sources": gaussian(seeds[4], (GROUPS, C, NSRC), 1.0, 6.0, ((0, 8), (1, 16))),
        "ext_map": draw_ext_map(jax.random.fold_in(seeds[8], 71), 0),
        "parent_front": draw_parent_front(jax.random.fold_in(seeds[8], 71), 0),
        "parent_rhs": gaussian(seeds[7], (NP, NSRC), 1.0, 6.0, ((0, 128),), jnp.float32),
    }


def reference(pivot_inverse, cross_block, contrib_block, pivot_sources, contrib_sources, ext_map, parent_front, parent_rhs):
    def one_front(running, members):
        parent, right_side = running
        inverse, coupling, contrib, piv_source, con_source, targets = members
        lower_part = jnp.dot(coupling, inverse.T, preferred_element_type=jnp.float32).astype(jnp.bfloat16)
        schur_rows = contrib - jnp.dot(lower_part, lower_part.T, preferred_element_type=jnp.float32)
        solved = jnp.dot(inverse, piv_source, preferred_element_type=jnp.float32).astype(jnp.bfloat16)
        update = con_source.astype(jnp.float32) - jnp.dot(lower_part, solved, preferred_element_type=jnp.float32)
        parent = parent.at[targets[:, None], targets[None, :]].add(schur_rows)
        right_side = right_side.at[targets].add(update)
        return (parent, right_side), solved

    (front_out, rhs_out), solved = lax.scan(
        one_front, (parent_front, parent_rhs),
        (pivot_inverse, cross_block, contrib_block, pivot_sources, contrib_sources, ext_map))
    return solved, front_out, rhs_out
```

```python
import functools

import jax
import jax.numpy as jnp
from jax import lax
from jax.experimental import pallas as pl
from jax.experimental.pallas import tpu as pltpu
from jax.sharding import PartitionSpec as P

MESH = pl.DeviceIdType.MESH
F32, BF16, I32 = jnp.float32, jnp.bfloat16, jnp.int32
NT = (((1,), (1,)), ((), ()))
NN = (((1,), (0,)), ((), ()))


def dot(a, b, dims=NN):
    return lax.dot_general(a, b, dims, preferred_element_type=F32)


def hbm():
    return pl.BlockSpec(memory_space=pl.ANY)


def vmem():
    return pl.BlockSpec(memory_space=pltpu.VMEM)


def onehot(ids, n):
    return (lax.broadcasted_iota(I32, (n, ids.shape[1]), 0) == ids).astype(F32).astype(BF16)


def strict(n):
    r = lax.broadcasted_iota(I32, (n, n), 0)
    c = lax.broadcasted_iota(I32, (n, n), 1)
    return (r < c).astype(F32).astype(BF16)


def joined(parts):
    r = lax.broadcasted_iota(I32, (224, 896), 0)
    c = lax.broadcasted_iota(I32, (224, 896), 1)
    total = jnp.zeros((8, 896), F32)
    for b in range(4):
        shift = (c == r + 224 * b).astype(F32).astype(BF16)
        total = total + dot(parts[b].astype(F32).astype(BF16), shift)
    return total.astype(I32)


def places(member):
    mb = member.astype(BF16)
    before = dot(mb, strict(128))
    count = dot(mb, jnp.ones((128, 128), BF16)).astype(BF16)
    r = lax.broadcasted_iota(I32, (64, 64), 0)
    c = lax.broadcasted_iota(I32, (64, 64), 1)
    above = dot((c < r).astype(F32).astype(BF16), count)
    row_count = dot(jnp.ones((8, 128), BF16), mb, NT).astype(BF16)
    starts = dot(row_count, strict(64))
    return (before + above).astype(I32), starts.astype(I32)


def main_kernel(
    inv, cross, contrib, csrc, psrc, emap,
    arrived, index, start, target, solved_own,
    invf, srcb, low, la, lb, cbuf, sent, held, solved_all, moved, select, slots, outs, mapsb,
    loc_sem, ms, mr, zs, zr, xs, xr, cs, cr, ls, lr, es, er,
):
    g = lax.axis_index("grp")
    h = lax.axis_index("hlp")
    z, x = h // 4, lax.rem(h, 4)
    me = g * 16 + h

    def at(dz, dx):
        return lax.rem(z + dz + 4, 4) * 4 + lax.rem(x + dx + 4, 4)

    def chunks(block):
        return block // 2 + 1

    def each(count, fn, first=0):
        def body(c, carry):
            fn(c)
            return carry

        lax.fori_loop(first, count, body, 0)

    def remote(source, target, ssem, rsem, to):
        return pltpu.make_async_remote_copy(
            source, target, ssem, rsem, device_id={"hlp": to}, device_id_type=MESH
        )

    def wait(ref, sem):
        pltpu.make_async_copy(ref, ref, sem).wait()

    def who(grp, i):
        return lax.rem(grp + g, 8), lax.rem(h + i, 16)

    barrier = pltpu.get_barrier_semaphore()

    def greet(i):
        p = lax.rem(me + i, 128)
        pl.semaphore_signal(barrier, inc=1, device_id=(p // 16, lax.rem(p, 16)), device_id_type=MESH)

    each(128, greet, 1)
    own = pltpu.make_async_copy(inv, invf.at[h], loc_sem.at[0])
    load = pltpu.make_async_copy(contrib, cbuf, loc_sem.at[1])
    load.start()

    def clear(i):
        def chunk(c):
            invf[i, :, pl.ds(pl.multiple_of(c * 256, 256), 256)] = jnp.zeros((128, 256), BF16)

        each(8, chunk, chunks(i))

    each(16, clear)
    own.start()
    mapsb[pl.ds(pl.multiple_of(me * 8, 8), 8), :] = emap[...]
    for b in range(4):
        @pl.when(z == b)
        def _():
            srcb[b, x] = psrc[:, 128 * b : 128 * (b + 1)]

    load.wait()
    for b in range(4):
        sent[b, :, 0:896] = cbuf[:, 896 * b : 896 * (b + 1)].astype(BF16)
        sent[b, :, 896:1024] = csrc[:, 128 * b : 128 * (b + 1)]
    own.wait()
    pl.semaphore_wait(barrier, 127)

    def piece(block, c, part=None):
        cols = pl.ds(pl.multiple_of(c * 256, 256), 256)
        if part is None:
            return invf.at[block, :, cols]
        return invf.at[block, pl.ds(64 * part, 64), cols]

    def map_rows(first, count):
        return mapsb.at[pl.ds(pl.multiple_of(first * 8, 8), count * 8), :]

    def send_z(c):
        remote(piece(h, c), piece(h, c), zs.at[0, c], zr.at[0, c], at(1, 0)).start()
        remote(piece(h, c), piece(h, c), zs.at[1, c], zr.at[1, c], at(-1, 0)).start()

    def send_x(r, block):
        def go(c):
            remote(piece(block, c), piece(block, c), xs.at[r, 0, c], xr.at[r, 0, c], at(0, 1)).start()
            remote(piece(block, c), piece(block, c), xs.at[r, 1, c], xr.at[r, 1, c], at(0, -1)).start()

        return go

    def pass_z(block, d, step):
        def go(c):
            wait(piece(block, c), zr.at[d, c])
            remote(
                piece(block, c, d), piece(block, c, d), zs.at[2 + d, c], zr.at[2 + d, c], at(step, 0)
            ).start()

        return go

    offsets = (0, -1, 1, 2)

    def pass_x(r):
        for d, dx in ((0, -1), (1, 1)):
            block = at(offsets[r], dx)

            def go(c, d=d, dx=dx, block=block):
                wait(piece(block, c), xr.at[r, d, c])
                remote(
                    piece(block, c, d), piece(block, c, d), xs.at[r, 2 + d, c], xr.at[r, 2 + d, c], at(0, -dx)
                ).start()

            each(chunks(block), go)

    for i in (1, 2, 3):
        remote(map_rows(me, 1), map_rows(me, 1), ms.at[0, i], mr.at[0, i], at(0, i)).start()
    each(chunks(h), send_z)
    each(chunks(h), send_x(0, h))
    for i in (1, 2, 3):
        to = lax.rem(z + i, 4)
        cols = pl.ds(pl.multiple_of(to * 128, 128), 128)
        remote(psrc.at[:, cols], srcb.at[z, x], cs.at[0, i], cr.at[0, i], at(i, 0)).start()
    for i in (1, 2, 3):
        wait(map_rows(me, 1), mr.at[0, i])
    line = g * 16 + z * 4
    for i in (1, 2, 3):
        remote(map_rows(line, 4), map_rows(line, 4), ms.at[1, i], mr.at[1, i], at(i, 0)).start()

    def first(c):
        pass_z(at(-1, 0), 0, 1)(c)
        send_x(1, at(-1, 0))(c)

    def second(c):
        pass_z(at(1, 0), 1, -1)(c)
        send_x(2, at(1, 0))(c)

    each(chunks(at(-1, 0)), first)
    each(chunks(at(1, 0)), second)
    for i in (1, 2, 3):
        to = lax.rem(z + i, 4)
        remote(sent.at[to], held.at[z], cs.at[1, i], cr.at[1, i], at(i, 0)).start()
    own_sent = pltpu.make_async_copy(sent.at[z], held.at[z], loc_sem.at[2])
    own_sent.start()
    for i in (1, 2, 3):
        wait(map_rows(line, 4), mr.at[1, i])
    for i in range(1, 8):
        pltpu.make_async_remote_copy(
            map_rows(g * 16, 16), map_rows(g * 16, 16), ms.at[2, i], mr.at[2, i],
            device_id=(lax.rem(g + i, 8), h), device_id_type=MESH,
        ).start()
    pass_x(0)
    for i in (1, 2, 3):
        wait(srcb.at[z, x], cr.at[0, i])
    for i in (1, 2, 3):
        remote(srcb.at[:, x], srcb.at[:, x], cs.at[2, i], cr.at[2, i], at(0, i)).start()

    def third(c):
        wait(piece(at(2, 0), c, 0), zr.at[2, c])
        wait(piece(at(2, 0), c, 1), zr.at[3, c])
        send_x(3, at(2, 0))(c)

    each(chunks(at(2, 0)), third)
    pass_x(1)

    rings = ((la, z, 1, 0), (lb, x, 0, 1))

    def slab(r, dz=0):
        return pl.ds(pl.multiple_of(lax.rem(z + dz + offsets[r] + 4, 4) * 512, 512), 512)

    def lpart(ref, i, part, r, dz=0):
        return ref.at[i, pl.ds(112 * part, 112), slab(r, dz)]

    def factor(r):
        block = at(offsets[r], 2)

        def arrive(c):
            wait(piece(block, c, 0), xr.at[r, 2, c])
            wait(piece(block, c, 1), xr.at[r, 3, c])

        each(chunks(block), arrive)
        zz = lax.rem(z + offsets[r] + 4, 4)
        for part in range(2):
            m = 2 * zz + part
            rows = invf[pl.ds(2 * m, 2)].reshape(256, 2048)
            low[:, pl.ds(pl.multiple_of(m * 256, 256), 256)] = dot(cross[...], rows, NT).astype(BF16)
        for order in (0, 1):
            for a, (ref, mine, dz, dx) in enumerate(rings):
                for d, step in ((0, 1), (1, -1)):
                    part = order if d == 0 else 1 - order
                    remote(
                        low.at[pl.ds(112 * part, 112), slab(r)], lpart(ref, mine, part, r),
                        ls.at[a, d, part, r], lr.at[a, d, part, r], at(dz * step, dx * step),
                    ).start()

    def factor_pass(r):
        for a, (ref, mine, dz, dx) in enumerate(rings):
            for d, step in ((0, 1), (1, -1)):
                block = lax.rem(mine - step + 4, 4)
                part = lpart(ref, block, d, r, -dz * step)
                wait(part, lr.at[a, d, d, r])
                remote(part, part, ls.at[a, 2, d, r], lr.at[a, 2, d, r], at(dz * step, dx * step)).start()

    factor(0)
    pass_x(2)
    factor(1)
    factor_pass(0)
    pass_x(3)

    own_maps = [mapsb[pl.ds(pl.multiple_of((line + b) * 8, 8), 8), :] for b in range(4)]
    high = onehot(joined([v // 128 for v in own_maps])[0:1], 64)
    lows = onehot(joined([lax.rem(v, 128) for v in own_maps])[0:1], 128)
    place, _ = places(dot(high, lows, NT))
    rank = jnp.zeros((1, 896), I32)
    for value, scale in ((place // 128, 128), (lax.rem(place, 128), 1)):
        found = dot(value.astype(F32).astype(BF16), lows) * high.astype(F32)
        rank = rank + jnp.sum(found, axis=0, keepdims=True).astype(I32) * scale
    select[...] = onehot(rank, 896)

    owners, slot_ids = [], []
    for k in range(4):
        owner = mapsb[pl.ds(pl.multiple_of((g * 16 + 4 * k + x) * 8, 8), 8), :] // 56
        hot = onehot(owner[0:1], 128)
        earlier = dot(hot, strict(224)) * hot.astype(F32)
        pos = jnp.sum(earlier, axis=0, keepdims=True).astype(I32)
        owners.append(owner)
        slot_ids.append(jnp.broadcast_to(pos + 3 * k, (8, 224)))
    owner, slot = joined(owners)[0:1], joined(slot_ids)[0:1]
    slots[0:1] = owner * 16 + slot
    for q in range(3):
        slots[q + 1 : q + 2] = jnp.where(slot // 4 == q, owner * 16 + 12 + lax.rem(slot, 4), -1)

    factor(2)
    factor_pass(1)
    for i in (1, 2, 3):
        wait(srcb.at[:, x], cr.at[2, i])
    factor(3)
    factor_pass(2)
    sources = srcb[...].reshape(2048, 128)

    def solve(m):
        rows = invf[pl.ds(2 * m, 2)].reshape(256, 2048)
        solved_all[pl.ds(pl.multiple_of(m * 256, 256), 256), :] = dot(rows, sources).astype(BF16)

    each(8, solve)
    for i in (1, 2, 3):
        to = at(i, 0)
        remote(
            solved_all.at[pl.ds(pl.multiple_of(to * 128, 128), 128), :], solved_own.at[z],
            cs.at[3, i], cr.at[3, i], to,
        ).start()
    own_s = pltpu.make_async_copy(
        solved_all.at[pl.ds(pl.multiple_of(h * 128, 128), 128), :], solved_own.at[z], loc_sem.at[3]
    )
    own_s.start()
    la[z] = low[...]
    lb[x] = low[...]
    factor_pass(3)
    for i in (1, 2, 3):
        wait(held.at[z], cr.at[1, i])
    own_sent.wait()
    for r in range(4):
        for a, (ref, mine, dz, dx) in enumerate(rings):
            for d, step in ((0, 1), (1, -1)):
                block = lax.rem(mine - step + 4, 4)
                wait(lpart(ref, block, 1 - d, r, -dz * step), lr.at[a, d, 1 - d, r])
                wait(lpart(ref, lax.rem(mine + 2, 4), d, r, 2 * dz), lr.at[a, 2, d, r])

    def rows_of(k):
        left = la[k]
        got = (held[k, :, 0:896].astype(F32) - dot(left, lb[...].reshape(896, 2048), NT)).astype(BF16)
        moved[k, :, 0:896] = dot(got, select[...], NT).astype(BF16)
        moved[k, :, 896:1024] = (held[k, :, 896:1024].astype(F32) - dot(left, solved_all[...])).astype(BF16)

    each(4, rows_of)

    def send_rows(j):
        grp = lax.rem(g + j, 8)
        row = lax.broadcasted_iota(I32, (256, 896), 0) + grp * 256
        main = (row == slots[0:1]).astype(F32).astype(BF16)
        last = moved[:, :, 768:1024].reshape(896, 256)
        for q in range(3):
            extra = (row == slots[q + 1 : q + 2]).astype(F32).astype(BF16)
            part = dot(main, moved[:, :, 256 * q : 256 * (q + 1)].reshape(896, 256)) + dot(extra, last)
            outs[pl.ds(grp * 16, 16), :, 256 * q : 256 * (q + 1)] = part.astype(BF16).reshape(16, 16, 256)

        def go(i):
            to = lax.rem(h + i, 16)

            @pl.when((j != 0) | (i != 0))
            def _():
                pltpu.make_async_remote_copy(
                    outs.at[grp * 16 + to], arrived.at[me], es, er, device_id=(grp, to), device_id_type=MESH
                ).start()

        each(16, go)

    each(8, send_rows)
    own_rows = pltpu.make_async_copy(outs.at[me], arrived.at[me], loc_sem.at[4])
    own_rows.start()

    for i in range(1, 8):
        wait(map_rows(0, 16), mr.at[2, i])

    def table(i):
        member = jnp.zeros((64, 128), F32)
        for b in range(4):
            v = mapsb[pl.ds(pl.multiple_of((4 * i + b) * 8, 8), 8), :][0:1]
            member = member + dot(onehot(v // 128, 64), onehot(lax.rem(v, 128), 128), NT)
        place, starts = places(member)
        index[i] = jnp.where(member > 0.5, lax.rem(place, 128), -1)[:56]
        start[i] = jnp.minimum(starts, 895)

    each(32, table)
    every = mapsb[...]
    r = lax.broadcasted_iota(I32, (128, 1024), 0)
    c = lax.broadcasted_iota(I32, (128, 1024), 1)
    eighth = (c == 8 * r).astype(F32).astype(BF16)
    mine = (every // 56 == me).astype(F32)
    local = dot(eighth, ((lax.rem(every, 56) + 1).astype(F32) * mine).astype(BF16))
    mine = dot(eighth, mine.astype(BF16))
    pos = dot(mine.astype(BF16), strict(224))
    r = lax.broadcasted_iota(I32, (128, 64), 0)
    c = lax.broadcasted_iota(I32, (128, 64), 1)
    keep = lax.broadcasted_iota(I32, (8, 128), 1) // 16 == lax.broadcasted_iota(I32, (8, 128), 0)
    totals = [jnp.zeros((8, 64), F32) for _ in range(4)]
    for p in range(3):
        found = jnp.where(pos == p, local, 0.0).astype(BF16)
        line_of = dot(jnp.ones((8, 224), BF16), found, NT)
        line_of = jnp.where(keep, line_of, 0.0).astype(BF16)
        slot_of = 3 * lax.rem(r // 4, 4) + p
        for v in range(4):
            want = slot_of if v == 0 else slot_of - 4 * (v - 1) + 12
            fits = (lax.rem(r, 4) == c // 16) & (want == lax.rem(c, 16))
            if v > 0:
                fits = fits & (lax.rem(c, 16) >= 12)
            totals[v] = totals[v] + dot(line_of, fits.astype(F32).astype(BF16))
    for v in range(4):
        target[v] = totals[v].astype(I32) - 1

    def sent_z(c):
        for d in (0, 1):
            wait(piece(h, c), zs.at[d, c])

    each(chunks(h), sent_z)
    for d, dz in ((0, -1), (1, 1)):

        def sent_pass(c, d=d, dz=dz):
            wait(piece(at(dz, 0), c, d), zs.at[2 + d, c])

        each(chunks(at(dz, 0)), sent_pass)
    for r in range(4):

        def sent_x(c, r=r):
            for d in (0, 1):
                wait(piece(at(offsets[r], 0), c), xs.at[r, d, c])

        each(chunks(at(offsets[r], 0)), sent_x)
        for d, dx in ((0, -1), (1, 1)):

            def sent_pass_x(c, r=r, d=d, dx=dx):
                wait(piece(at(offsets[r], dx), c, d), xs.at[r, 2 + d, c])

            each(chunks(at(offsets[r], dx)), sent_pass_x)
    for i in (1, 2, 3):
        wait(map_rows(me, 1), ms.at[0, i])
        wait(map_rows(line, 4), ms.at[1, i])
        wait(srcb.at[z, x], cs.at[0, i])
        wait(held.at[z], cs.at[1, i])
        wait(srcb.at[:, x], cs.at[2, i])
        wait(solved_own.at[z], cs.at[3, i])
        wait(solved_own.at[z], cr.at[3, i])
    for i in range(1, 8):
        wait(map_rows(0, 16), ms.at[2, i])
    for r in range(4):
        for a, (ref, mine_at, dz, dx) in enumerate(rings):
            for d in (0, 1):
                for part in (0, 1):
                    wait(lpart(ref, mine_at, part, r), ls.at[a, d, part, r])
                wait(lpart(ref, mine_at, d, r), ls.at[a, 2, d, r])
    own_s.wait()
    own_rows.wait()
    some = pl.ds(0, 127)
    wait(outs.at[some], es)
    wait(arrived.at[some], er)


def main_call(inv, cross, contrib, csrc, psrc, emap):
    dma = pltpu.SemaphoreType.DMA
    return pl.pallas_call(
        main_kernel,
        out_shape=(
            jax.ShapeDtypeStruct((128, 16, 768), BF16),
            jax.ShapeDtypeStruct((32, 56, 128), I32),
            jax.ShapeDtypeStruct((32, 8, 64), I32),
            jax.ShapeDtypeStruct((4, 8, 64), I32),
            jax.ShapeDtypeStruct((4, 128, 128), BF16),
        ),
        in_specs=[hbm(), vmem(), hbm(), vmem(), vmem(), vmem()],
        out_specs=(hbm(), vmem(), vmem(), vmem(), hbm()),
        scratch_shapes=[
            pltpu.VMEM((16, 128, 2048), BF16),
            pltpu.VMEM((4, 4, 128, 128), BF16),
            pltpu.VMEM((224, 2048), BF16),
            pltpu.VMEM((4, 224, 2048), BF16),
            pltpu.VMEM((4, 224, 2048), BF16),
            pltpu.VMEM((224, 3584), F32),
            pltpu.VMEM((4, 224, 1024), BF16),
            pltpu.VMEM((4, 224, 1024), BF16),
            pltpu.VMEM((2048, 128), BF16),
            pltpu.VMEM((4, 224, 1024), BF16),
            pltpu.VMEM((896, 896), BF16),
            pltpu.VMEM((8, 896), I32),
            pltpu.VMEM((128, 16, 768), BF16),
            pltpu.VMEM((1024, 224), I32),
            dma((5,)),
            dma((3, 8)), dma((3, 8)),
            dma((4, 8)), dma((4, 8)),
            dma((4, 4, 8)), dma((4, 4, 8)),
            dma((4, 4)), dma((4, 4)),
            dma((2, 3, 2, 4)), dma((2, 3, 2, 4)),
            dma, dma,
        ],
        compiler_params=pltpu.CompilerParams(
            collective_id=0, has_side_effects=True, vmem_limit_bytes=56 << 20
        ),
        name="fronts",
    )(inv, cross, contrib, csrc, psrc, emap)


def spread_kernel(start, target, index, rows, parent, rhs, front, right, tile):
    i = pl.program_id(0)

    @pl.when(i == 0)
    def _():
        front[...] = parent[...]
        right[...] = rhs[...]

    row = lax.broadcasted_iota(I32, (56, 64), 0)
    pick = [(row == target[v, 0]).astype(F32).astype(BF16) for v in range(4)]
    tail = jnp.zeros((56, 256), F32)
    for q in range(3):
        got = rows[0, :, 256 * q : 256 * (q + 1)]
        main = dot(pick[0], got)
        tile[2 * q] = main[:, :128]
        tile[2 * q + 1] = main[:, 128:]
        tail = tail + dot(pick[q + 1], got)
    tile[6] = tail[:, :128]
    tile[7] = tail[:, 128:]
    which = lax.rem(i, 4)
    for zz in range(4):

        @pl.when(which == zz)
        def _():
            right[:, 128 * zz : 128 * (zz + 1)] += tail[:, 128:]

    lane = lax.broadcasted_iota(I32, (56, 128), 1)
    for t in range(56):
        at = start[i, t]
        j = at // 128
        both = jnp.where(lane >= lax.rem(at, 128), tile[j], tile[j + 1])
        where = jnp.broadcast_to(index[0, t : t + 1], (56, 128))
        taken = jnp.take_along_axis(both, where & 127, axis=1)
        front[:, 128 * t : 128 * (t + 1)] += jnp.where(where >= 0, taken, 0.0)


def spread(start, target, index, rows, parent, rhs):
    whole = lambda shape: pl.BlockSpec(shape, lambda i: (0,) * len(shape))
    return pl.pallas_call(
        spread_kernel,
        grid=(32,),
        out_shape=(
            jax.ShapeDtypeStruct((56, 7168), F32),
            jax.ShapeDtypeStruct((56, 512), F32),
        ),
        in_specs=[
            pl.BlockSpec(memory_space=pltpu.SMEM),
            pl.BlockSpec((4, 1, 1, 64), lambda i: (0, i // 4, 0, 0)),
            pl.BlockSpec((1, 56, 128), lambda i: (i, 0, 0)),
            pl.BlockSpec((1, 64, 768), lambda i: (i, 0, 0)),
            whole((56, 7168)),
            whole((56, 512)),
        ],
        out_specs=(whole((56, 7168)), whole((56, 512))),
        scratch_shapes=[pltpu.VMEM((8, 56, 128), F32)],
        compiler_params=pltpu.CompilerParams(vmem_limit_bytes=40 << 20),
        name="spread",
    )(start, target, index, rows, parent, rhs)


def on_device(
    pivot_inverse, cross_block, contrib_block, pivot_sources, contrib_sources, ext_map, parent_front, parent_rhs
):
    emap = jnp.broadcast_to(ext_map, (8, 224))
    arrived, index, start, target, solved_own = main_call(
        pivot_inverse[0], cross_block[0], contrib_block[0], contrib_sources[0], pivot_sources[0], emap
    )
    solved = solved_own.transpose(1, 0, 2).reshape(1, 128, 512)
    front, right = spread(
        start[:, 0, :], target.reshape(4, 8, 1, 64), index, arrived.reshape(32, 64, 768), parent_front, parent_rhs
    )
    return solved, front, right


def solution(mesh):
    return jax.shard_map(
        on_device,
        mesh=mesh,
        in_specs=(
            P("grp", "hlp", None),
            P("grp", "hlp", None),
            P("grp", "hlp", None),
            P("grp", "hlp", None),
            P("grp", "hlp", None),
            P("grp", "hlp"),
            P(("grp", "hlp"), None),
            P(("grp", "hlp"), None),
        ),
        out_specs=(P("grp", "hlp", None), P(("grp", "hlp"), None), P(("grp", "hlp"), None)),
        check_vma=False,
    )
```

```python
import functools

import jax
import jax.numpy as jnp
from jax import lax
from jax.experimental import pallas as pl
from jax.experimental.pallas import tpu as pltpu
from jax.sharding import PartitionSpec as P

MESH = pl.DeviceIdType.MESH
F32, BF16, I32 = jnp.float32, jnp.bfloat16, jnp.int32
NT = (((1,), (1,)), ((), ()))
NN = (((1,), (0,)), ((), ()))
UNROLL = 8


def dot(a, b, dims=NN):
    return lax.dot_general(a, b, dims, preferred_element_type=F32)


def hbm():
    return pl.BlockSpec(memory_space=pl.ANY)


def vmem():
    return pl.BlockSpec(memory_space=pltpu.VMEM)


def onehot(ids, n):
    return (lax.broadcasted_iota(I32, (n, ids.shape[1]), 0) == ids).astype(F32).astype(BF16)


def onehot_rows(ids):
    return (lax.broadcasted_iota(I32, (56, ids.shape[1]), 0) == ids).astype(F32).astype(BF16)


def strict(n):
    r = lax.broadcasted_iota(I32, (n, n), 0)
    c = lax.broadcasted_iota(I32, (n, n), 1)
    return (r < c).astype(F32).astype(BF16)


def joined(parts):
    r = lax.broadcasted_iota(I32, (224, 896), 0)
    c = lax.broadcasted_iota(I32, (224, 896), 1)
    total = jnp.zeros((8, 896), F32)
    for b in range(4):
        shift = (c == r + 224 * b).astype(F32).astype(BF16)
        total = total + dot(parts[b].astype(F32).astype(BF16), shift)
    return total.astype(I32)


def places(member):
    mb = member.astype(BF16)
    before = dot(mb, strict(128))
    count = dot(mb, jnp.ones((128, 128), BF16)).astype(BF16)
    r = lax.broadcasted_iota(I32, (64, 64), 0)
    c = lax.broadcasted_iota(I32, (64, 64), 1)
    above = dot((c < r).astype(F32).astype(BF16), count)
    row_count = dot(jnp.ones((8, 128), BF16), mb, NT).astype(BF16)
    starts = dot(row_count, strict(64))
    return (before + above).astype(I32), starts.astype(I32)


def main_kernel(
    inv, cross, contrib, csrc, psrc, emap, parent, rhs,
    front, right, solved_own,
    invf, srcb, low, la, lb, cbuf, sent, held, solved_all, moved, select, slots, outs, mapsb,
    arrived, index, start, start_at, target, tile,
    loc_sem, ms, mr, zs, zr, xs, xr, cs, cr, ls, lr, es, er,
):
    g = lax.axis_index("grp")
    h = lax.axis_index("hlp")
    z, x = h // 4, lax.rem(h, 4)
    me = g * 16 + h

    def at(dz, dx):
        return lax.rem(z + dz + 4, 4) * 4 + lax.rem(x + dx + 4, 4)

    def chunks(block):
        return block // 2 + 1

    def each(count, fn, first=0):
        def body(c, carry):
            fn(c)
            return carry

        lax.fori_loop(first, count, body, 0)

    def remote(source, target, ssem, rsem, to):
        return pltpu.make_async_remote_copy(
            source, target, ssem, rsem, device_id={"hlp": to}, device_id_type=MESH
        )

    def wait(ref, sem):
        pltpu.make_async_copy(ref, ref, sem).wait()

    def who(grp, i):
        return lax.rem(grp + g, 8), lax.rem(h + i, 16)

    barrier = pltpu.get_barrier_semaphore()

    def greet(i):
        p = lax.rem(me + i, 128)
        pl.semaphore_signal(barrier, inc=1, device_id=(p // 16, lax.rem(p, 16)), device_id_type=MESH)

    each(128, greet, 1)
    own = pltpu.make_async_copy(inv, invf.at[h], loc_sem.at[0])
    load = pltpu.make_async_copy(contrib, cbuf, loc_sem.at[1])
    load.start()
    base = (
        pltpu.make_async_copy(parent, front, loc_sem.at[5]),
        pltpu.make_async_copy(rhs, right, loc_sem.at[6]),
    )
    for copy in base:
        copy.start()

    def clear(i):
        def chunk(c):
            invf[i, :, pl.ds(pl.multiple_of(c * 256, 256), 256)] = jnp.zeros((128, 256), BF16)

        each(8, chunk, chunks(i))

    each(16, clear)
    own.start()
    mapsb[pl.ds(pl.multiple_of(me * 8, 8), 8), :] = emap[...]
    for b in range(4):
        @pl.when(z == b)
        def _():
            srcb[b, x] = psrc[:, 128 * b : 128 * (b + 1)]

    load.wait()
    for b in range(4):
        sent[b, :, 0:896] = cbuf[:, 896 * b : 896 * (b + 1)].astype(BF16)
        sent[b, :, 896:1024] = csrc[:, 128 * b : 128 * (b + 1)]
    own.wait()
    pl.semaphore_wait(barrier, 127)

    def piece(block, c, part=None):
        cols = pl.ds(pl.multiple_of(c * 256, 256), 256)
        if part is None:
            return invf.at[block, :, cols]
        return invf.at[block, pl.ds(64 * part, 64), cols]

    def map_rows(first, count):
        return mapsb.at[pl.ds(pl.multiple_of(first * 8, 8), count * 8), :]

    def send_z(c):
        remote(piece(h, c), piece(h, c), zs.at[0, c], zr.at[0, c], at(1, 0)).start()
        remote(piece(h, c), piece(h, c), zs.at[1, c], zr.at[1, c], at(-1, 0)).start()

    def send_x(r, block):
        def go(c):
            remote(piece(block, c), piece(block, c), xs.at[r, 0, c], xr.at[r, 0, c], at(0, 1)).start()
            remote(piece(block, c), piece(block, c), xs.at[r, 1, c], xr.at[r, 1, c], at(0, -1)).start()

        return go

    def pass_z(block, d, step):
        def go(c):
            wait(piece(block, c), zr.at[d, c])
            remote(
                piece(block, c, d), piece(block, c, d), zs.at[2 + d, c], zr.at[2 + d, c], at(step, 0)
            ).start()

        return go

    offsets = (0, -1, 1, 2)

    def pass_x(r):
        for d, dx in ((0, -1), (1, 1)):
            block = at(offsets[r], dx)

            def go(c, d=d, dx=dx, block=block):
                wait(piece(block, c), xr.at[r, d, c])
                remote(
                    piece(block, c, d), piece(block, c, d), xs.at[r, 2 + d, c], xr.at[r, 2 + d, c], at(0, -dx)
                ).start()

            each(chunks(block), go)

    for i in (1, 2, 3):
        remote(map_rows(me, 1), map_rows(me, 1), ms.at[0, i], mr.at[0, i], at(0, i)).start()
    each(chunks(h), send_z)
    each(chunks(h), send_x(0, h))
    for i in (1, 2, 3):
        to = lax.rem(z + i, 4)
        cols = pl.ds(pl.multiple_of(to * 128, 128), 128)
        remote(psrc.at[:, cols], srcb.at[z, x], cs.at[0, i], cr.at[0, i], at(i, 0)).start()
    for i in (1, 2, 3):
        wait(map_rows(me, 1), mr.at[0, i])
    line = g * 16 + z * 4
    for i in (1, 2, 3):
        remote(map_rows(line, 4), map_rows(line, 4), ms.at[1, i], mr.at[1, i], at(i, 0)).start()

    def first(c):
        pass_z(at(-1, 0), 0, 1)(c)
        send_x(1, at(-1, 0))(c)

    def second(c):
        pass_z(at(1, 0), 1, -1)(c)
        send_x(2, at(1, 0))(c)

    each(chunks(at(-1, 0)), first)
    each(chunks(at(1, 0)), second)
    for i in (1, 2, 3):
        to = lax.rem(z + i, 4)
        remote(sent.at[to], held.at[z], cs.at[1, i], cr.at[1, i], at(i, 0)).start()
    own_sent = pltpu.make_async_copy(sent.at[z], held.at[z], loc_sem.at[2])
    own_sent.start()
    for i in (1, 2, 3):
        wait(map_rows(line, 4), mr.at[1, i])
    for i in range(1, 8):
        pltpu.make_async_remote_copy(
            map_rows(g * 16, 16), map_rows(g * 16, 16), ms.at[2, i], mr.at[2, i],
            device_id=(lax.rem(g + i, 8), h), device_id_type=MESH,
        ).start()
    pass_x(0)
    for i in (1, 2, 3):
        wait(srcb.at[z, x], cr.at[0, i])
    for i in (1, 2, 3):
        remote(srcb.at[:, x], srcb.at[:, x], cs.at[2, i], cr.at[2, i], at(0, i)).start()

    def third(c):
        wait(piece(at(2, 0), c, 0), zr.at[2, c])
        wait(piece(at(2, 0), c, 1), zr.at[3, c])
        send_x(3, at(2, 0))(c)

    each(chunks(at(2, 0)), third)
    pass_x(1)

    rings = ((la, z, 1, 0), (lb, x, 0, 1))

    def slab(r, dz=0):
        return pl.ds(pl.multiple_of(lax.rem(z + dz + offsets[r] + 4, 4) * 512, 512), 512)

    def lpart(ref, i, part, r, dz=0):
        return ref.at[i, pl.ds(112 * part, 112), slab(r, dz)]

    def factor(r):
        block = at(offsets[r], 2)

        def arrive(c):
            wait(piece(block, c, 0), xr.at[r, 2, c])
            wait(piece(block, c, 1), xr.at[r, 3, c])

        each(chunks(block), arrive)
        zz = lax.rem(z + offsets[r] + 4, 4)
        for part in range(2):
            m = 2 * zz + part
            rows = invf[pl.ds(2 * m, 2)].reshape(256, 2048)
            low[:, pl.ds(pl.multiple_of(m * 256, 256), 256)] = dot(cross[...], rows, NT).astype(BF16)
        for order in (0, 1):
            for a, (ref, mine, dz, dx) in enumerate(rings):
                for d, step in ((0, 1), (1, -1)):
                    part = order if d == 0 else 1 - order
                    remote(
                        low.at[pl.ds(112 * part, 112), slab(r)], lpart(ref, mine, part, r),
                        ls.at[a, d, part, r], lr.at[a, d, part, r], at(dz * step, dx * step),
                    ).start()

    def factor_pass(r):
        for a, (ref, mine, dz, dx) in enumerate(rings):
            for d, step in ((0, 1), (1, -1)):
                block = lax.rem(mine - step + 4, 4)
                part = lpart(ref, block, d, r, -dz * step)
                wait(part, lr.at[a, d, d, r])
                remote(part, part, ls.at[a, 2, d, r], lr.at[a, 2, d, r], at(dz * step, dx * step)).start()

    def table(i):
        member = jnp.zeros((64, 128), F32)
        for b in range(4):
            v = mapsb[pl.ds(pl.multiple_of((4 * i + b) * 8, 8), 8), :][0:1]
            member = member + dot(onehot(v // 128, 64), onehot(lax.rem(v, 128), 128), NT)
        place, starts = places(member)
        index[i] = jnp.where(member > 0.5, lax.rem(place, 128), -1)[:56]
        start[i] = jnp.clip(starts, 0, 895)

    factor(0)
    for i in range(1, 8):
        wait(map_rows(0, 16), mr.at[2, i])
    each(8, table)
    pass_x(2)
    factor(1)
    factor_pass(0)
    each(16, table, 8)
    pass_x(3)

    own_maps = [mapsb[pl.ds(pl.multiple_of((line + b) * 8, 8), 8), :] for b in range(4)]
    high = onehot(joined([v // 128 for v in own_maps])[0:1], 64)
    lows = onehot(joined([lax.rem(v, 128) for v in own_maps])[0:1], 128)
    place, _ = places(dot(high, lows, NT))
    rank = jnp.zeros((1, 896), I32)
    for value, scale in ((place // 128, 128), (lax.rem(place, 128), 1)):
        found = dot(value.astype(F32).astype(BF16), lows) * high.astype(F32)
        rank = rank + jnp.sum(found, axis=0, keepdims=True).astype(I32) * scale
    select[...] = onehot(rank, 896)

    owners, slot_ids = [], []
    for k in range(4):
        owner = mapsb[pl.ds(pl.multiple_of((g * 16 + 4 * k + x) * 8, 8), 8), :] // 56
        hot = onehot(owner[0:1], 128)
        earlier = dot(hot, strict(224)) * hot.astype(F32)
        pos = jnp.sum(earlier, axis=0, keepdims=True).astype(I32)
        owners.append(owner)
        slot_ids.append(jnp.broadcast_to(pos + 3 * k, (8, 224)))
    owner, slot = joined(owners)[0:1], joined(slot_ids)[0:1]
    slots[0:1] = owner * 16 + slot
    for q in range(3):
        slots[q + 1 : q + 2] = jnp.where(slot // 4 == q, owner * 16 + 12 + lax.rem(slot, 4), -1)

    factor(2)
    factor_pass(1)
    each(24, table, 16)
    for i in (1, 2, 3):
        wait(srcb.at[:, x], cr.at[2, i])
    factor(3)
    factor_pass(2)
    sources = srcb[...].reshape(2048, 128)

    def solve(m):
        rows = invf[pl.ds(2 * m, 2)].reshape(256, 2048)
        solved_all[pl.ds(pl.multiple_of(m * 256, 256), 256), :] = dot(rows, sources).astype(BF16)

    each(8, solve)
    for i in (1, 2, 3):
        to = at(i, 0)
        remote(
            solved_all.at[pl.ds(pl.multiple_of(to * 128, 128), 128), :], solved_own.at[z],
            cs.at[3, i], cr.at[3, i], to,
        ).start()
    own_s = pltpu.make_async_copy(
        solved_all.at[pl.ds(pl.multiple_of(h * 128, 128), 128), :], solved_own.at[z], loc_sem.at[3]
    )
    own_s.start()
    la[z] = low[...]
    lb[x] = low[...]
    each(32, table, 24)
    starts_in = pltpu.make_async_copy(start, start_at, loc_sem.at[7])
    starts_in.start()

    every = mapsb[...]
    r = lax.broadcasted_iota(I32, (128, 1024), 0)
    c = lax.broadcasted_iota(I32, (128, 1024), 1)
    eighth = (c == 8 * r).astype(F32).astype(BF16)
    mine = (every // 56 == me).astype(F32)
    local = dot(eighth, ((lax.rem(every, 56) + 1).astype(F32) * mine).astype(BF16))
    mine = dot(eighth, mine.astype(BF16))
    pos = dot(mine.astype(BF16), strict(224))
    r = lax.broadcasted_iota(I32, (128, 64), 0)
    c = lax.broadcasted_iota(I32, (128, 64), 1)
    keep = lax.broadcasted_iota(I32, (8, 128), 1) // 16 == lax.broadcasted_iota(I32, (8, 128), 0)
    totals = [jnp.zeros((8, 64), F32) for _ in range(4)]
    for p in range(3):
        found = jnp.where(pos == p, local, 0.0).astype(BF16)
        line_of = dot(jnp.ones((8, 224), BF16), found, NT)
        line_of = jnp.where(keep, line_of, 0.0).astype(BF16)
        slot_of = 3 * lax.rem(r // 4, 4) + p
        for v in range(4):
            want = slot_of if v == 0 else slot_of - 4 * (v - 1) + 12
            fits = (lax.rem(r, 4) == c // 16) & (want == lax.rem(c, 16))
            if v > 0:
                fits = fits & (lax.rem(c, 16) >= 12)
            totals[v] = totals[v] + dot(line_of, fits.astype(F32).astype(BF16))
    for v in range(4):
        target[v] = totals[v].astype(I32) - 1

    factor_pass(3)
    for i in (1, 2, 3):
        wait(held.at[z], cr.at[1, i])
    own_sent.wait()
    for r in range(4):
        for a, (ref, mine, dz, dx) in enumerate(rings):
            for d, step in ((0, 1), (1, -1)):
                block = lax.rem(mine - step + 4, 4)
                wait(lpart(ref, block, 1 - d, r, -dz * step), lr.at[a, d, 1 - d, r])
                wait(lpart(ref, lax.rem(mine + 2, 4), d, r, 2 * dz), lr.at[a, 2, d, r])

    def rows_of(k):
        left = la[k]
        got = (held[k, :, 0:896].astype(F32) - dot(left, lb[...].reshape(896, 2048), NT)).astype(BF16)
        moved[k, :, 0:896] = dot(got, select[...], NT).astype(BF16)
        moved[k, :, 896:1024] = (held[k, :, 896:1024].astype(F32) - dot(left, solved_all[...])).astype(BF16)

    each(4, rows_of)

    def send_rows(j, first=0):
        grp = lax.rem(g + j, 8)
        row = lax.broadcasted_iota(I32, (256, 896), 0) + grp * 256
        main = (row == slots[0:1]).astype(F32).astype(BF16)
        last = moved[:, :, 768:1024].reshape(896, 256)
        for q in range(3):
            extra = (row == slots[q + 1 : q + 2]).astype(F32).astype(BF16)
            part = dot(main, moved[:, :, 256 * q : 256 * (q + 1)].reshape(896, 256)) + dot(extra, last)
            outs[pl.ds(grp * 16, 16), :, 256 * q : 256 * (q + 1)] = part.astype(BF16).reshape(16, 16, 256)

        def go(i):
            to = lax.rem(h + i, 16)

            pltpu.make_async_remote_copy(
                outs.at[grp * 16 + to], arrived.at[me], es, er.at[g], device_id=(grp, to), device_id_type=MESH
            ).start()

        each(16, go, first)

    send_rows(0, 1)
    own_rows = pltpu.make_async_copy(outs.at[me], arrived.at[me], er.at[g])
    own_rows.start()
    each(8, send_rows, 1)


    starts_in.wait()
    for copy in base:
        copy.wait()

    def spread(j):
        grp = lax.rem(g + 8 - j, 8)
        wait(arrived.at[pl.ds(grp * 16, 16)], er.at[grp])
        pick = [onehot_rows(target[v, pl.ds(grp, 1), :]) for v in range(4)]
        for b in range(4):
            got = arrived[pl.ds(grp * 16 + 4 * b, 4)].reshape(64, 768)
            tail = jnp.zeros((56, 256), F32)
            for q in range(3):
                part = dot(pick[0], got[:, 256 * q : 256 * (q + 1)])
                tile[b, 2 * q] = part[:, :128]
                tile[b, 2 * q + 1] = part[:, 128:]
                tail = tail + dot(pick[q + 1], got[:, 256 * q : 256 * (q + 1)])
            tile[b, 6] = tail[:, :128]
            tile[b, 7] = tail[:, 128:]
            right[:, 128 * b : 128 * (b + 1)] += tail[:, 128:]
        lane = lax.broadcasted_iota(I32, (56, 128), 1)

        def columns(s):
            for u in range(UNROLL):
                t = s * UNROLL + u
                cols = pl.ds(pl.multiple_of(t * 128, 128), 128)
                total = front[:, cols]
                for b in range(4):
                    begin = start_at[grp * 4 + b, 0, t]
                    i = jnp.clip(begin // 128, 0, 6)
                    both = jnp.where(lane >= lax.rem(begin, 128), tile[b, i], tile[b, i + 1])
                    where = jnp.broadcast_to(index[grp * 4 + b, pl.ds(t, 1), :], (56, 128))
                    taken = jnp.take_along_axis(both, where & 127, axis=1)
                    total = total + jnp.where(where >= 0, taken, 0.0)
                front[:, cols] = total

        each(56 // UNROLL, columns)

    each(8, spread)

    def sent_z(c):
        for d in (0, 1):
            wait(piece(h, c), zs.at[d, c])

    each(chunks(h), sent_z)
    for d, dz in ((0, -1), (1, 1)):

        def sent_pass(c, d=d, dz=dz):
            wait(piece(at(dz, 0), c, d), zs.at[2 + d, c])

        each(chunks(at(dz, 0)), sent_pass)
    for r in range(4):

        def sent_x(c, r=r):
            for d in (0, 1):
                wait(piece(at(offsets[r], 0), c), xs.at[r, d, c])

        each(chunks(at(offsets[r], 0)), sent_x)
        for d, dx in ((0, -1), (1, 1)):

            def sent_pass_x(c, r=r, d=d, dx=dx):
                wait(piece(at(offsets[r], dx), c, d), xs.at[r, 2 + d, c])

            each(chunks(at(offsets[r], dx)), sent_pass_x)
    for i in (1, 2, 3):
        wait(map_rows(me, 1), ms.at[0, i])
        wait(map_rows(line, 4), ms.at[1, i])
        wait(srcb.at[z, x], cs.at[0, i])
        wait(held.at[z], cs.at[1, i])
        wait(srcb.at[:, x], cs.at[2, i])
        wait(solved_own.at[z], cs.at[3, i])
        wait(solved_own.at[z], cr.at[3, i])
    for i in range(1, 8):
        wait(map_rows(0, 16), ms.at[2, i])
    for r in range(4):
        for a, (ref, mine_at, dz, dx) in enumerate(rings):
            for d in (0, 1):
                for part in (0, 1):
                    wait(lpart(ref, mine_at, part, r), ls.at[a, d, part, r])
                wait(lpart(ref, mine_at, d, r), ls.at[a, 2, d, r])
    own_s.wait()
    wait(outs.at[pl.ds(0, 127)], es)


def main_call(inv, cross, contrib, csrc, psrc, emap, parent, rhs):
    dma = pltpu.SemaphoreType.DMA
    return pl.pallas_call(
        main_kernel,
        out_shape=(
            jax.ShapeDtypeStruct((56, 7168), F32),
            jax.ShapeDtypeStruct((56, 512), F32),
            jax.ShapeDtypeStruct((4, 128, 128), BF16),
        ),
        in_specs=[hbm(), vmem(), hbm(), vmem(), vmem(), vmem(), hbm(), hbm()],
        out_specs=(vmem(), vmem(), hbm()),
        scratch_shapes=[
            pltpu.VMEM((16, 128, 2048), BF16),
            pltpu.VMEM((4, 4, 128, 128), BF16),
            pltpu.VMEM((224, 2048), BF16),
            pltpu.VMEM((4, 224, 2048), BF16),
            pltpu.VMEM((4, 224, 2048), BF16),
            pltpu.VMEM((224, 3584), F32),
            pltpu.VMEM((4, 224, 1024), BF16),
            pltpu.VMEM((4, 224, 1024), BF16),
            pltpu.VMEM((2048, 128), BF16),
            pltpu.VMEM((4, 224, 1024), BF16),
            pltpu.VMEM((896, 896), BF16),
            pltpu.VMEM((8, 896), I32),
            pltpu.VMEM((128, 16, 768), BF16),
            pltpu.VMEM((1024, 224), I32),
            pltpu.VMEM((128, 16, 768), BF16),
            pltpu.VMEM((32, 56, 128), I32),
            pltpu.VMEM((32, 8, 64), I32),
            pltpu.SMEM((32, 8, 64), I32),
            pltpu.VMEM((4, 8, 64), I32),
            pltpu.VMEM((4, 8, 56, 128), F32),
            dma((8,)),
            dma((3, 8)), dma((3, 8)),
            dma((4, 8)), dma((4, 8)),
            dma((4, 4, 8)), dma((4, 4, 8)),
            dma((4, 4)), dma((4, 4)),
            dma((2, 3, 2, 4)), dma((2, 3, 2, 4)),
            dma, dma((8,)),
        ],
        compiler_params=pltpu.CompilerParams(
            collective_id=0, has_side_effects=True, vmem_limit_bytes=58 << 20
        ),
        name="fronts",
    )(inv, cross, contrib, csrc, psrc, emap, parent, rhs)


def on_device(
    pivot_inverse, cross_block, contrib_block, pivot_sources, contrib_sources, ext_map, parent_front, parent_rhs
):
    front, right, solved_own = main_call(
        pivot_inverse[0], cross_block[0], contrib_block[0], contrib_sources[0], pivot_sources[0],
        jnp.broadcast_to(ext_map, (8, 224)), parent_front, parent_rhs,
    )
    return solved_own.transpose(1, 0, 2).reshape(1, 128, 512), front, right


def solution(mesh):
    return jax.shard_map(
        on_device,
        mesh=mesh,
        in_specs=(
            P("grp", "hlp", None),
            P("grp", "hlp", None),
            P("grp", "hlp", None),
            P("grp", "hlp", None),
            P("grp", "hlp", None),
            P("grp", "hlp"),
            P(("grp", "hlp"), None),
            P(("grp", "hlp"), None),
        ),
        out_specs=(P("grp", "hlp", None), P(("grp", "hlp"), None), P(("grp", "hlp"), None)),
        check_vma=False,
    )
```

```python
import functools

import jax
import jax.numpy as jnp
from jax import lax
from jax.experimental import pallas as pl
from jax.experimental.pallas import tpu as pltpu
from jax.sharding import PartitionSpec as P

MESH = pl.DeviceIdType.MESH
F32, BF16, I32 = jnp.float32, jnp.bfloat16, jnp.int32
NT = (((1,), (1,)), ((), ()))
NN = (((1,), (0,)), ((), ()))
UNROLL = 14


def dot(a, b, dims=NN):
    return lax.dot_general(a, b, dims, preferred_element_type=F32)


def hbm():
    return pl.BlockSpec(memory_space=pl.ANY)


def vmem():
    return pl.BlockSpec(memory_space=pltpu.VMEM)


def onehot(ids, n):
    return (lax.broadcasted_iota(I32, (n, ids.shape[1]), 0) == ids).astype(F32).astype(BF16)


def onehot_rows(ids):
    return (lax.broadcasted_iota(I32, (56, ids.shape[1]), 0) == ids).astype(F32).astype(BF16)


def strict(n):
    r = lax.broadcasted_iota(I32, (n, n), 0)
    c = lax.broadcasted_iota(I32, (n, n), 1)
    return (r < c).astype(F32).astype(BF16)


def joined(parts):
    r = lax.broadcasted_iota(I32, (224, 896), 0)
    c = lax.broadcasted_iota(I32, (224, 896), 1)
    total = jnp.zeros((8, 896), F32)
    for b in range(4):
        shift = (c == r + 224 * b).astype(F32).astype(BF16)
        total = total + dot(parts[b].astype(F32).astype(BF16), shift)
    return total.astype(I32)


def places(member):
    mb = member.astype(BF16)
    before = dot(mb, strict(128))
    count = dot(mb, jnp.ones((128, 128), BF16)).astype(BF16)
    r = lax.broadcasted_iota(I32, (64, 64), 0)
    c = lax.broadcasted_iota(I32, (64, 64), 1)
    above = dot((c < r).astype(F32).astype(BF16), count)
    row_count = dot(jnp.ones((8, 128), BF16), mb, NT).astype(BF16)
    starts = dot(row_count, strict(64))
    return (before + above).astype(I32), starts.astype(I32)


def main_kernel(
    inv, cross, contrib, csrc, psrc, emap, parent, rhs,
    front, right, solved_own,
    invf, srcb, low, la, lb, cbuf, sent, held, solved_all, moved, select, slots, outs, mapsb,
    arrived, index, start, start_at, target, tile, via, vs, vr,
    loc_sem, ms, mr, zs, zr, xs, xr, cs, cr, ls, lr, es, er,
):
    g = lax.axis_index("grp")
    h = lax.axis_index("hlp")
    z, x = h // 4, lax.rem(h, 4)
    me = g * 16 + h

    def at(dz, dx):
        return lax.rem(z + dz + 4, 4) * 4 + lax.rem(x + dx + 4, 4)

    def chunks(block):
        return block // 2 + 1

    def each(count, fn, first=0):
        def body(c, carry):
            fn(c)
            return carry

        lax.fori_loop(first, count, body, 0)

    def remote(source, target, ssem, rsem, to):
        return pltpu.make_async_remote_copy(
            source, target, ssem, rsem, device_id={"hlp": to}, device_id_type=MESH
        )

    def wait(ref, sem):
        pltpu.make_async_copy(ref, ref, sem).wait()

    def who(grp, i):
        return lax.rem(grp + g, 8), lax.rem(h + i, 16)

    barrier = pltpu.get_barrier_semaphore()

    def greet(i):
        p = lax.rem(me + i, 128)
        pl.semaphore_signal(barrier, inc=1, device_id=(p // 16, lax.rem(p, 16)), device_id_type=MESH)

    each(128, greet, 1)
    own = pltpu.make_async_copy(inv, invf.at[h], loc_sem.at[0])
    load = pltpu.make_async_copy(contrib, cbuf, loc_sem.at[1])
    load.start()
    base = (
        pltpu.make_async_copy(parent, front, loc_sem.at[5]),
        pltpu.make_async_copy(rhs, right, loc_sem.at[6]),
    )
    for copy in base:
        copy.start()

    def clear(i):
        def chunk(c):
            invf[i, :, pl.ds(pl.multiple_of(c * 256, 256), 256)] = jnp.zeros((128, 256), BF16)

        each(8, chunk, chunks(i))

    each(16, clear)
    own.start()
    mapsb[pl.ds(pl.multiple_of(me * 8, 8), 8), :] = jnp.broadcast_to(emap[...], (8, 224))
    for b in range(4):
        @pl.when(z == b)
        def _():
            srcb[b, x] = psrc[:, 128 * b : 128 * (b + 1)]

    load.wait()
    for b in range(4):
        sent[b, :, 0:896] = cbuf[:, 896 * b : 896 * (b + 1)].astype(BF16)
        sent[b, :, 896:1024] = csrc[:, 128 * b : 128 * (b + 1)]
    own.wait()
    pl.semaphore_wait(barrier, 127)

    def sized(block, fn):
        for n in range(1, 9):
            pl.when(chunks(block) == n)(functools.partial(fn, 256 * n))

    def piece(block, n, part):
        return invf.at[block, pl.ds(64 * part, 64), pl.ds(0, n)]

    def map_rows(first, count):
        return mapsb.at[pl.ds(pl.multiple_of(first * 8, 8), count * 8), :]

    def send(block, part, ssem, rsem, to):
        def go(n):
            ref = piece(block, n, part)
            remote(ref, ref, ssem, rsem, to).start()

        sized(block, go)

    def await_piece(block, part, sem):
        sized(block, lambda n: wait(piece(block, n, part), sem))

    def send_both(block, ssem, rsem, right, left, parts):
        def go(n):
            for p in parts:
                for d, to in ((0, right), (1, left)):
                    part = p if d == 0 or len(parts) == 1 else 1 - p
                    ref = piece(block, n, part)
                    remote(ref, ref, ssem.at[d, part], rsem.at[d, part], to).start()

        sized(block, go)

    offsets = (0, -1, 1, 2)

    def send_x(r, parts=(0, 1)):
        send_both(at(offsets[r], 0), xs.at[r], xr.at[r], at(0, 1), at(0, -1), parts)

    def pass_x(r):
        for d, dx in ((0, -1), (1, 1)):
            block = at(offsets[r], dx)

            def go(n, d=d, dx=dx, block=block):
                ref = piece(block, n, d)
                wait(ref, xr.at[r, d, d])
                remote(ref, ref, xs.at[r, 2 + d, 0], xr.at[r, 2 + d, 0], at(0, -dx)).start()

            sized(block, go)

    for i in (1, 2, 3):
        remote(map_rows(me, 1), map_rows(me, 1), ms.at[0, i], mr.at[0, i], at(0, i)).start()
    send_both(h, zs, zr, at(1, 0), at(-1, 0), (0, 1))
    send_x(0)
    for i in (1, 2, 3):
        to = lax.rem(z + i, 4)
        cols = pl.ds(pl.multiple_of(to * 128, 128), 128)
        remote(psrc.at[:, cols], srcb.at[z, x], cs.at[0, i], cr.at[0, i], at(i, 0)).start()
    for i in (1, 2, 3):
        wait(map_rows(me, 1), mr.at[0, i])
    line = g * 16 + z * 4
    for i in (1, 2, 3):
        remote(map_rows(line, 4), map_rows(line, 4), ms.at[1, i], mr.at[1, i], at(i, 0)).start()

    for d, dz in ((0, -1), (1, 1)):
        block = at(dz, 0)
        await_piece(block, d, zr.at[d, d])
        send(block, d, zs.at[2 + d, 0], zr.at[2 + d, 0], at(-dz, 0))
        send_x(1 + d, (d,))
    for d, dz in ((0, -1), (1, 1)):
        await_piece(at(dz, 0), 1 - d, zr.at[d, 1 - d])
        send_x(1 + d, (1 - d,))
    for d, i in ((0, 1), (1, 3)):
        part = pl.ds(112 * d, 112)
        remote(sent.at[lax.rem(z + 2, 4), part, :], via.at[d], vs.at[0, d], vr.at[0, d], at(i, 0)).start()
    for i in (1, 3):
        remote(sent.at[lax.rem(z + i, 4)], held.at[z], cs.at[1, i], cr.at[1, i], at(i, 0)).start()
    own_sent = pltpu.make_async_copy(sent.at[z], held.at[z], loc_sem.at[2])
    own_sent.start()
    for i in (1, 2, 3):
        wait(map_rows(line, 4), mr.at[1, i])
    for i in range(1, 8):
        pltpu.make_async_remote_copy(
            map_rows(g * 16, 16), map_rows(g * 16, 16), ms.at[2, i], mr.at[2, i],
            device_id=(lax.rem(g + i, 8), h), device_id_type=MESH,
        ).start()
    pass_x(0)
    for i in (1, 2, 3):
        wait(srcb.at[z, x], cr.at[0, i])
    for i in (1, 3):
        remote(srcb.at[:, x], srcb.at[:, x], cs.at[2, i], cr.at[2, i], at(0, i)).start()

    for d in (0, 1):
        await_piece(at(2, 0), d, zr.at[2 + d, 0])
        send_x(3, (d,))
    pass_x(1)

    rings = ((la, z, 1, 0), (lb, x, 0, 1))

    def slab(r, dz=0):
        return pl.ds(pl.multiple_of(lax.rem(z + dz + offsets[r] + 4, 4) * 512, 512), 512)

    def lpart(ref, i, part, r, dz=0):
        return ref.at[i, pl.ds(112 * part, 112), slab(r, dz)]

    def factor(r):
        block = at(offsets[r], 2)

        await_piece(at(offsets[r], -1), 1, xr.at[r, 0, 1])
        await_piece(at(offsets[r], 1), 0, xr.at[r, 1, 0])
        await_piece(block, 0, xr.at[r, 2, 0])
        await_piece(block, 1, xr.at[r, 3, 0])
        zz = lax.rem(z + offsets[r] + 4, 4)
        for part in range(2):
            m = 2 * zz + part
            rows = invf[pl.ds(2 * m, 2)].reshape(256, 2048)
            low[:, pl.ds(pl.multiple_of(m * 256, 256), 256)] = dot(cross[...], rows, NT).astype(BF16)
        for order in (0, 1):
            for a, (ref, mine, dz, dx) in enumerate(rings):
                for d, step in ((0, 1), (1, -1)):
                    part = order if d == 0 else 1 - order
                    remote(
                        low.at[pl.ds(112 * part, 112), slab(r)], lpart(ref, mine, part, r),
                        ls.at[a, d, part, r], lr.at[a, d, part, r], at(dz * step, dx * step),
                    ).start()

    def factor_pass(r):
        for a, (ref, mine, dz, dx) in enumerate(rings):
            for d, step in ((0, 1), (1, -1)):
                block = lax.rem(mine - step + 4, 4)
                part = lpart(ref, block, d, r, -dz * step)
                wait(part, lr.at[a, d, d, r])
                remote(part, part, ls.at[a, 2, d, r], lr.at[a, 2, d, r], at(dz * step, dx * step)).start()

    def table(i):
        member = jnp.zeros((64, 128), F32)
        for b in range(4):
            v = mapsb[pl.ds(pl.multiple_of((4 * i + b) * 8, 8), 8), :][0:1]
            member = member + dot(onehot(v // 128, 64), onehot(lax.rem(v, 128), 128), NT)
        place, starts = places(member)
        index[i] = jnp.where(member > 0.5, lax.rem(place, 128), -1)[:56]
        start[i] = jnp.clip(starts, 0, 895)

    for d, i in ((0, 1), (1, 3)):
        wait(via.at[d], vr.at[0, d])
        origin = lax.rem(z + 4 - i, 4)
        remote(
            via.at[d], held.at[origin, pl.ds(112 * d, 112), :], vs.at[1, d], vr.at[1, d], at(i, 0)
        ).start()
    factor(0)
    for i in range(1, 8):
        wait(map_rows(0, 16), mr.at[2, i])
    each(8, table)
    pass_x(2)
    for d, i in ((0, 1), (1, 3)):
        wait(srcb.at[:, x], cr.at[2, i])
        ref = srcb.at[pl.ds(2 * d, 2), lax.rem(x + 4 - i, 4)]
        remote(ref, ref, vs.at[2, d], vr.at[2, d], at(0, i)).start()
    factor(1)
    factor_pass(0)
    each(16, table, 8)
    pass_x(3)

    own_maps = [mapsb[pl.ds(pl.multiple_of((line + b) * 8, 8), 8), :] for b in range(4)]
    high = onehot(joined([v // 128 for v in own_maps])[0:1], 64)
    lows = onehot(joined([lax.rem(v, 128) for v in own_maps])[0:1], 128)
    place, _ = places(dot(high, lows, NT))
    rank = jnp.zeros((1, 896), I32)
    for value, scale in ((place // 128, 128), (lax.rem(place, 128), 1)):
        found = dot(value.astype(F32).astype(BF16), lows) * high.astype(F32)
        rank = rank + jnp.sum(found, axis=0, keepdims=True).astype(I32) * scale
    select[...] = onehot(rank, 896)

    owners, slot_ids = [], []
    for k in range(4):
        owner = mapsb[pl.ds(pl.multiple_of((g * 16 + 4 * k + x) * 8, 8), 8), :] // 56
        hot = onehot(owner[0:1], 128)
        earlier = dot(hot, strict(224)) * hot.astype(F32)
        pos = jnp.sum(earlier, axis=0, keepdims=True).astype(I32)
        owners.append(owner)
        slot_ids.append(jnp.broadcast_to(pos + 3 * k, (8, 224)))
    owner, slot = joined(owners)[0:1], joined(slot_ids)[0:1]
    slots[0:1] = owner * 16 + slot

    factor(2)
    factor_pass(1)
    each(24, table, 16)
    for d in (0, 1):
        ref = srcb.at[pl.ds(2 * d, 2), x]
        wait(ref, vr.at[2, d])
    factor(3)
    factor_pass(2)
    sources = srcb[...].reshape(2048, 128)

    own_part = solved_own.at[:, pl.ds(pl.multiple_of(z * 128, 128), 128)]

    def solve(m):
        rows = invf[pl.ds(2 * m, 2)].reshape(256, 2048)
        solved_all[pl.ds(pl.multiple_of(m * 256, 256), 256), :] = dot(rows, sources).astype(BF16)

    each(8, solve)
    for i in (1, 2, 3):
        to = at(i, 0)
        remote(
            solved_all.at[pl.ds(pl.multiple_of(to * 128, 128), 128), :], own_part,
            cs.at[3, i], cr.at[3, i], to,
        ).start()
    own_s = pltpu.make_async_copy(
        solved_all.at[pl.ds(pl.multiple_of(h * 128, 128), 128), :], own_part, loc_sem.at[3]
    )
    own_s.start()
    la[z] = low[...]
    lb[x] = low[...]
    each(32, table, 24)
    starts_in = pltpu.make_async_copy(start, start_at, loc_sem.at[7])
    starts_in.start()

    every = mapsb[...]
    r = lax.broadcasted_iota(I32, (128, 1024), 0)
    c = lax.broadcasted_iota(I32, (128, 1024), 1)
    eighth = (c == 8 * r).astype(F32).astype(BF16)
    mine = (every // 56 == me).astype(F32)
    local = dot(eighth, ((lax.rem(every, 56) + 1).astype(F32) * mine).astype(BF16))
    mine = dot(eighth, mine.astype(BF16))
    pos = dot(mine.astype(BF16), strict(224))
    r = lax.broadcasted_iota(I32, (128, 64), 0)
    c = lax.broadcasted_iota(I32, (128, 64), 1)
    keep = lax.broadcasted_iota(I32, (8, 128), 1) // 16 == lax.broadcasted_iota(I32, (8, 128), 0)
    totals = [jnp.zeros((8, 64), F32) for _ in range(4)]
    for p in range(3):
        found = jnp.where(pos == p, local, 0.0).astype(BF16)
        line_of = dot(jnp.ones((8, 224), BF16), found, NT)
        line_of = jnp.where(keep, line_of, 0.0).astype(BF16)
        slot_of = 3 * lax.rem(r // 4, 4) + p
        for v in range(4):
            want = slot_of if v == 0 else slot_of - 4 * (v - 1) + 12
            fits = (lax.rem(r, 4) == c // 16) & (want == lax.rem(c, 16))
            if v > 0:
                fits = fits & (lax.rem(c, 16) >= 12)
            totals[v] = totals[v] + dot(line_of, fits.astype(F32).astype(BF16))
    for v in range(4):
        target[v] = totals[v].astype(I32) - 1

    factor_pass(3)
    for i in (1, 3):
        wait(held.at[z], cr.at[1, i])
    for d in (0, 1):
        wait(via.at[d], vr.at[1, d])
    own_sent.wait()
    for r in range(4):
        for a, (ref, mine, dz, dx) in enumerate(rings):
            for d, step in ((0, 1), (1, -1)):
                block = lax.rem(mine - step + 4, 4)
                wait(lpart(ref, block, 1 - d, r, -dz * step), lr.at[a, d, 1 - d, r])
                wait(lpart(ref, lax.rem(mine + 2, 4), d, r, 2 * dz), lr.at[a, 2, d, r])

    def rows_of(k):
        left = la[k]
        got = (held[k, :, 0:896].astype(F32) - dot(left, lb[...].reshape(896, 2048), NT)).astype(BF16)
        moved[k, :, 0:896] = dot(got, select[...], NT).astype(BF16)
        moved[k, :, 896:1024] = (held[k, :, 896:1024].astype(F32) - dot(left, solved_all[...])).astype(BF16)

    each(4, rows_of)

    def send_rows(j, first=0):
        grp = lax.rem(g + j, 8)
        row = lax.broadcasted_iota(I32, (256, 896), 0) + grp * 256
        main = (row == slots[0:1]).astype(F32).astype(BF16)
        def quarter(q):
            cols = moved[:, :, 256 * q : 256 * (q + 1)].reshape(896, 256)
            return dot(main, cols).reshape(16, 2, 8, 256)

        last = quarter(3)
        free = lax.broadcasted_iota(I32, (16, 8, 256), 1) >= 4
        turned = [jnp.concatenate([last[:, t, 4:], last[:, t, :4]], axis=1) for t in range(2)]
        for q, extra in enumerate((turned[0], last[:, 0], turned[1])):
            part = quarter(q)
            both = jnp.concatenate([part[:, 0], jnp.where(free, extra, part[:, 1])], axis=1)
            outs[pl.ds(grp * 16, 16), :, 256 * q : 256 * (q + 1)] = both.astype(BF16)

        def go(i):
            to = lax.rem(h + i, 16)

            pltpu.make_async_remote_copy(
                outs.at[grp * 16 + to], arrived.at[me], es, er.at[g], device_id=(grp, to), device_id_type=MESH
            ).start()

        each(16, go, first)

    send_rows(0, 1)
    own_rows = pltpu.make_async_copy(outs.at[me], arrived.at[me], er.at[g])
    own_rows.start()
    each(8, send_rows, 1)


    starts_in.wait()
    for copy in base:
        copy.wait()

    def spread(j):
        grp = lax.rem(g + 8 - j, 8)
        wait(arrived.at[pl.ds(grp * 16, 16)], er.at[grp])
        pick = [onehot_rows(target[v, pl.ds(grp, 1), :]) for v in range(4)]
        for b in range(4):
            got = arrived[pl.ds(grp * 16 + 4 * b, 4)].reshape(64, 768)
            tail = jnp.zeros((56, 256), F32)
            for q in range(3):
                part = dot(pick[0], got[:, 256 * q : 256 * (q + 1)])
                tile[b, 2 * q] = part[:, :128]
                tile[b, 2 * q + 1] = part[:, 128:]
                tail = tail + dot(pick[q + 1], got[:, 256 * q : 256 * (q + 1)])
            tile[b, 6] = tail[:, :128]
            tile[b, 7] = tail[:, 128:]
            right[:, 128 * b : 128 * (b + 1)] += tail[:, 128:]
        lane = lax.broadcasted_iota(I32, (56, 128), 1)

        def columns(s):
            for u in range(UNROLL):
                t = s * UNROLL + u
                cols = pl.ds(pl.multiple_of(t * 128, 128), 128)
                total = front[:, cols]
                for b in range(4):
                    begin = start_at[grp * 4 + b, 0, t]
                    i = jnp.clip(begin // 128, 0, 6)
                    both = jnp.where(lane >= lax.rem(begin, 128), tile[b, i], tile[b, i + 1])
                    where = jnp.broadcast_to(index[grp * 4 + b, pl.ds(t, 1), :], (56, 128))
                    taken = jnp.take_along_axis(both, where & 127, axis=1)
                    total = total + jnp.where(where >= 0, taken, 0.0)
                front[:, cols] = total

        each(56 // UNROLL, columns)

    each(8, spread)

    for d in (0, 1):
        for part in (0, 1):
            await_piece(h, part, zs.at[d, part])
            for r in range(4):
                await_piece(at(offsets[r], 0), part, xs.at[r, d, part])
        step = 2 * d - 1
        await_piece(at(step, 0), d, zs.at[2 + d, 0])
        for r in range(4):
            await_piece(at(offsets[r], step), d, xs.at[r, 2 + d, 0])
    for i in (1, 2, 3):
        wait(map_rows(me, 1), ms.at[0, i])
        wait(map_rows(line, 4), ms.at[1, i])
        wait(srcb.at[z, x], cs.at[0, i])
        if i != 2:
            wait(held.at[z], cs.at[1, i])
        if i != 2:
            wait(srcb.at[:, x], cs.at[2, i])
        wait(own_part, cs.at[3, i])
        wait(own_part, cr.at[3, i])
    for i in range(1, 8):
        wait(map_rows(0, 16), ms.at[2, i])
    for r in range(4):
        for a, (ref, mine_at, dz, dx) in enumerate(rings):
            for d in (0, 1):
                for part in (0, 1):
                    wait(lpart(ref, mine_at, part, r), ls.at[a, d, part, r])
                wait(lpart(ref, mine_at, d, r), ls.at[a, 2, d, r])
    for d in (0, 1):
        wait(via.at[d], vs.at[0, d])
        wait(via.at[d], vs.at[1, d])
        wait(srcb.at[pl.ds(2 * d, 2), x], vs.at[2, d])
    own_s.wait()
    wait(outs.at[pl.ds(0, 127)], es)


def main_call(inv, cross, contrib, csrc, psrc, emap, parent, rhs):
    dma = pltpu.SemaphoreType.DMA
    return pl.pallas_call(
        main_kernel,
        out_shape=(
            jax.ShapeDtypeStruct((56, 7168), F32),
            jax.ShapeDtypeStruct((56, 512), F32),
            jax.ShapeDtypeStruct((128, 512), BF16),
        ),
        in_specs=[hbm(), vmem(), hbm(), vmem(), vmem(), vmem(), hbm(), hbm()],
        out_specs=(vmem(), vmem(), hbm()),
        scratch_shapes=[
            pltpu.VMEM((16, 128, 2048), BF16),
            pltpu.VMEM((4, 4, 128, 128), BF16),
            pltpu.VMEM((224, 2048), BF16),
            pltpu.VMEM((4, 224, 2048), BF16),
            pltpu.VMEM((4, 224, 2048), BF16),
            pltpu.VMEM((224, 3584), F32),
            pltpu.VMEM((4, 224, 1024), BF16),
            pltpu.VMEM((4, 224, 1024), BF16),
            pltpu.VMEM((2048, 128), BF16),
            pltpu.VMEM((4, 224, 1024), BF16),
            pltpu.VMEM((896, 896), BF16),
            pltpu.VMEM((8, 896), I32),
            pltpu.VMEM((128, 16, 768), BF16),
            pltpu.VMEM((1024, 224), I32),
            pltpu.VMEM((128, 16, 768), BF16),
            pltpu.VMEM((32, 56, 128), I32),
            pltpu.VMEM((32, 8, 64), I32),
            pltpu.SMEM((32, 8, 64), I32),
            pltpu.VMEM((4, 8, 64), I32),
            pltpu.VMEM((4, 8, 56, 128), F32),
            pltpu.VMEM((2, 112, 1024), BF16),
            dma((3, 2)), dma((3, 2)),
            dma((8,)),
            dma((3, 8)), dma((3, 8)),
            dma((4, 2)), dma((4, 2)),
            dma((4, 4, 2)), dma((4, 4, 2)),
            dma((4, 4)), dma((4, 4)),
            dma((2, 3, 2, 4)), dma((2, 3, 2, 4)),
            dma, dma((8,)),
        ],
        compiler_params=pltpu.CompilerParams(
            collective_id=0, has_side_effects=True, vmem_limit_bytes=58 << 20
        ),
        name="fronts",
    )(inv, cross, contrib, csrc, psrc, emap, parent, rhs)


def on_device(
    pivot_inverse, cross_block, contrib_block, pivot_sources, contrib_sources, ext_map, parent_front, parent_rhs
):
    front, right, solved_own = main_call(
        pivot_inverse[0], cross_block[0], contrib_block[0], contrib_sources[0], pivot_sources[0],
        ext_map, parent_front, parent_rhs,
    )
    return solved_own[None], front, right


def solution(mesh):
    return jax.shard_map(
        on_device,
        mesh=mesh,
        in_specs=(
            P("grp", "hlp", None),
            P("grp", "hlp", None),
            P("grp", "hlp", None),
            P("grp", "hlp", None),
            P("grp", "hlp", None),
            P("grp", "hlp"),
            P(("grp", "hlp"), None),
            P(("grp", "hlp"), None),
        ),
        out_specs=(P("grp", "hlp", None), P(("grp", "hlp"), None), P(("grp", "hlp"), None)),
        check_vma=False,
    )
```

```python
import functools

import jax
import jax.numpy as jnp
from jax import lax
from jax.experimental import pallas as pl
from jax.experimental.pallas import tpu as pltpu
from jax.sharding import PartitionSpec as P

MESH = pl.DeviceIdType.MESH
F32, BF16, I32 = jnp.float32, jnp.bfloat16, jnp.int32
NT = (((1,), (1,)), ((), ()))
NN = (((1,), (0,)), ((), ()))
UNROLL = 14


def dot(a, b, dims=NN):
    return lax.dot_general(a, b, dims, preferred_element_type=F32)


def hbm():
    return pl.BlockSpec(memory_space=pl.ANY)


def vmem():
    return pl.BlockSpec(memory_space=pltpu.VMEM)


def onehot(ids, n):
    return (lax.broadcasted_iota(I32, (n, ids.shape[1]), 0) == ids).astype(F32).astype(BF16)


def onehot_rows(ids):
    return (lax.broadcasted_iota(I32, (56, ids.shape[1]), 0) == ids).astype(F32).astype(BF16)


def strict(n):
    r = lax.broadcasted_iota(I32, (n, n), 0)
    c = lax.broadcasted_iota(I32, (n, n), 1)
    return (r < c).astype(F32).astype(BF16)


def joined(parts):
    r = lax.broadcasted_iota(I32, (224, 896), 0)
    c = lax.broadcasted_iota(I32, (224, 896), 1)
    total = jnp.zeros((8, 896), F32)
    for b in range(4):
        shift = (c == r + 224 * b).astype(F32).astype(BF16)
        total = total + dot(parts[b].astype(F32).astype(BF16), shift)
    return total.astype(I32)


def places(member):
    mb = member.astype(BF16)
    before = dot(mb, strict(128))
    count = dot(mb, jnp.ones((128, 128), BF16)).astype(BF16)
    r = lax.broadcasted_iota(I32, (64, 64), 0)
    c = lax.broadcasted_iota(I32, (64, 64), 1)
    above = dot((c < r).astype(F32).astype(BF16), count)
    row_count = dot(jnp.ones((8, 128), BF16), mb, NT).astype(BF16)
    starts = dot(row_count, strict(64))
    return (before + above).astype(I32), starts.astype(I32)


def main_kernel(
    inv, cross, contrib, csrc, psrc, emap, parent, rhs,
    front, right, solved_own,
    invf, srcb, low, la, lb, cbuf, sent, held, solved_all, moved, select, slots, outs, mapsb,
    arrived, index, start, start_at, target, tile, via, vs, vr,
    loc_sem, ms, mr, zs, zr, xs, xr, cs, cr, ls, lr, es, er,
):
    g = lax.axis_index("grp")
    h = lax.axis_index("hlp")
    z, x = h // 4, lax.rem(h, 4)
    me = g * 16 + h

    def at(dz, dx):
        return lax.rem(z + dz + 4, 4) * 4 + lax.rem(x + dx + 4, 4)

    def chunks(block):
        return block // 2 + 1

    def each(count, fn, first=0):
        def body(c, carry):
            fn(c)
            return carry

        lax.fori_loop(first, count, body, 0)

    def remote(source, target, ssem, rsem, to):
        return pltpu.make_async_remote_copy(
            source, target, ssem, rsem, device_id={"hlp": to}, device_id_type=MESH
        )

    def wait(ref, sem):
        pltpu.make_async_copy(ref, ref, sem).wait()

    def who(grp, i):
        return lax.rem(grp + g, 8), lax.rem(h + i, 16)

    barrier = pltpu.get_barrier_semaphore()

    def greet(i):
        p = lax.rem(me + i, 128)
        pl.semaphore_signal(barrier, inc=1, device_id=(p // 16, lax.rem(p, 16)), device_id_type=MESH)

    each(128, greet, 1)
    own = pltpu.make_async_copy(inv, invf.at[h], loc_sem.at[0])
    load = pltpu.make_async_copy(contrib, cbuf, loc_sem.at[1])
    load.start()
    base = (
        pltpu.make_async_copy(parent, front, loc_sem.at[5]),
        pltpu.make_async_copy(rhs, right, loc_sem.at[6]),
    )
    for copy in base:
        copy.start()

    def clear(i):
        def chunk(c):
            invf[i, :, pl.ds(pl.multiple_of(c * 256, 256), 256)] = jnp.zeros((128, 256), BF16)

        each(8, chunk, chunks(i))

    each(16, clear)
    own.start()
    mapsb[pl.ds(pl.multiple_of(me * 8, 8), 8), :] = jnp.broadcast_to(emap[...], (8, 224))
    for b in range(4):
        @pl.when(z == b)
        def _():
            srcb[b, x] = psrc[:, 128 * b : 128 * (b + 1)]

    load.wait()
    for b in range(4):
        sent[b, :, 0:896] = cbuf[:, 896 * b : 896 * (b + 1)].astype(BF16)
        sent[b, :, 896:1024] = csrc[:, 128 * b : 128 * (b + 1)]
    own.wait()
    pl.semaphore_wait(barrier, 127)

    def sized(block, fn):
        for n in range(1, 9):
            pl.when(chunks(block) == n)(functools.partial(fn, 256 * n))

    def piece(block, n, part):
        return invf.at[block, pl.ds(64 * part, 64), pl.ds(0, n)]

    def map_rows(first, count):
        return mapsb.at[pl.ds(pl.multiple_of(first * 8, 8), count * 8), :]

    def send(block, part, ssem, rsem, to):
        def go(n):
            ref = piece(block, n, part)
            remote(ref, ref, ssem, rsem, to).start()

        sized(block, go)

    def await_piece(block, part, sem):
        sized(block, lambda n: wait(piece(block, n, part), sem))

    def send_both(block, ssem, rsem, right, left, parts):
        def go(n):
            for p in parts:
                for d, to in ((0, right), (1, left)):
                    part = p if d == 0 or len(parts) == 1 else 1 - p
                    ref = piece(block, n, part)
                    remote(ref, ref, ssem.at[d, part], rsem.at[d, part], to).start()

        sized(block, go)

    offsets = (0, -1, 1, 2)

    def send_x(r, parts=(0, 1)):
        send_both(at(offsets[r], 0), xs.at[r], xr.at[r], at(0, 1), at(0, -1), parts)

    def pass_x(r):
        for d, dx in ((0, -1), (1, 1)):
            block = at(offsets[r], dx)

            def go(n, d=d, dx=dx, block=block):
                ref = piece(block, n, d)
                wait(ref, xr.at[r, d, d])
                remote(ref, ref, xs.at[r, 2 + d, 0], xr.at[r, 2 + d, 0], at(0, -dx)).start()

            sized(block, go)

    for i in (1, 2, 3):
        remote(map_rows(me, 1), map_rows(me, 1), ms.at[0, i], mr.at[0, i], at(0, i)).start()
    send_both(h, zs, zr, at(1, 0), at(-1, 0), (0, 1))
    send_x(0)
    for i in (1, 2, 3):
        to = lax.rem(z + i, 4)
        cols = pl.ds(pl.multiple_of(to * 128, 128), 128)
        remote(psrc.at[:, cols], srcb.at[z, x], cs.at[0, i], cr.at[0, i], at(i, 0)).start()
    for i in (1, 2, 3):
        wait(map_rows(me, 1), mr.at[0, i])
    line = g * 16 + z * 4
    for i in (1, 2, 3):
        remote(map_rows(line, 4), map_rows(line, 4), ms.at[1, i], mr.at[1, i], at(i, 0)).start()

    for d, dz in ((0, -1), (1, 1)):
        block = at(dz, 0)
        await_piece(block, d, zr.at[d, d])
        send(block, d, zs.at[2 + d, 0], zr.at[2 + d, 0], at(-dz, 0))
        send_x(1 + d, (d,))
    for d, dz in ((0, -1), (1, 1)):
        await_piece(at(dz, 0), 1 - d, zr.at[d, 1 - d])
        send_x(1 + d, (1 - d,))
    for d, i in ((0, 1), (1, 3)):
        part = pl.ds(112 * d, 112)
        remote(sent.at[lax.rem(z + 2, 4), part, :], via.at[d], vs.at[0, d], vr.at[0, d], at(i, 0)).start()
    for i in (1, 3):
        remote(sent.at[lax.rem(z + i, 4)], held.at[z], cs.at[1, i], cr.at[1, i], at(i, 0)).start()
    own_sent = pltpu.make_async_copy(sent.at[z], held.at[z], loc_sem.at[2])
    own_sent.start()
    for i in (1, 2, 3):
        wait(map_rows(line, 4), mr.at[1, i])
    for i in range(1, 8):
        pltpu.make_async_remote_copy(
            map_rows(g * 16, 16), map_rows(g * 16, 16), ms.at[2, i], mr.at[2, i],
            device_id=(lax.rem(g + i, 8), h), device_id_type=MESH,
        ).start()
    pass_x(0)
    for i in (1, 2, 3):
        wait(srcb.at[z, x], cr.at[0, i])
    for i in (1, 3):
        remote(srcb.at[:, x], srcb.at[:, x], cs.at[2, i], cr.at[2, i], at(0, i)).start()

    for d in (0, 1):
        await_piece(at(2, 0), d, zr.at[2 + d, 0])
        send_x(3, (d,))
    pass_x(1)

    rings = ((la, z, 1, 0), (lb, x, 0, 1))

    def slab(r, dz=0):
        return pl.ds(pl.multiple_of(lax.rem(z + dz + offsets[r] + 4, 4) * 512, 512), 512)

    def lpart(ref, i, part, r, dz=0):
        return ref.at[i, pl.ds(112 * part, 112), slab(r, dz)]

    def factor(r):
        block = at(offsets[r], 2)

        await_piece(at(offsets[r], -1), 1, xr.at[r, 0, 1])
        await_piece(at(offsets[r], 1), 0, xr.at[r, 1, 0])
        await_piece(block, 0, xr.at[r, 2, 0])
        await_piece(block, 1, xr.at[r, 3, 0])
        zz = lax.rem(z + offsets[r] + 4, 4)
        for part in range(2):
            m = 2 * zz + part
            rows = invf[pl.ds(2 * m, 2)].reshape(256, 2048)
            low[:, pl.ds(pl.multiple_of(m * 256, 256), 256)] = dot(cross[...], rows, NT).astype(BF16)
        for order in (0, 1):
            for a, (ref, mine, dz, dx) in enumerate(rings):
                for d, step in ((0, 1), (1, -1)):
                    part = order if d == 0 else 1 - order
                    remote(
                        low.at[pl.ds(112 * part, 112), slab(r)], lpart(ref, mine, part, r),
                        ls.at[a, d, part, r], lr.at[a, d, part, r], at(dz * step, dx * step),
                    ).start()

    def factor_pass(r):
        for a, (ref, mine, dz, dx) in enumerate(rings):
            for d, step in ((0, 1), (1, -1)):
                block = lax.rem(mine - step + 4, 4)
                part = lpart(ref, block, d, r, -dz * step)
                wait(part, lr.at[a, d, d, r])
                remote(part, part, ls.at[a, 2, d, r], lr.at[a, 2, d, r], at(dz * step, dx * step)).start()

    def table(i):
        member = jnp.zeros((64, 128), F32)
        for b in range(4):
            v = mapsb[pl.ds(pl.multiple_of((4 * i + b) * 8, 8), 8), :][0:1]
            member = member + dot(onehot(v // 128, 64), onehot(lax.rem(v, 128), 128), NT)
        place, starts = places(member)
        index[i] = jnp.where(member > 0.5, lax.rem(place, 128), -1)[:56]
        start[i] = jnp.clip(starts, 0, 895)

    for d, i in ((0, 1), (1, 3)):
        wait(via.at[d], vr.at[0, d])
        origin = lax.rem(z + 4 - i, 4)
        remote(
            via.at[d], held.at[origin, pl.ds(112 * d, 112), :], vs.at[1, d], vr.at[1, d], at(i, 0)
        ).start()
    factor(0)
    for i in range(1, 8):
        wait(map_rows(0, 16), mr.at[2, i])
    each(8, table)
    pass_x(2)
    for d, i in ((0, 1), (1, 3)):
        wait(srcb.at[:, x], cr.at[2, i])
        ref = srcb.at[pl.ds(2 * d, 2), lax.rem(x + 4 - i, 4)]
        remote(ref, ref, vs.at[2, d], vr.at[2, d], at(0, i)).start()
    factor(1)
    factor_pass(0)
    each(16, table, 8)
    pass_x(3)

    own_maps = [mapsb[pl.ds(pl.multiple_of((line + b) * 8, 8), 8), :] for b in range(4)]
    high = onehot(joined([v // 128 for v in own_maps])[0:1], 64)
    lows = onehot(joined([lax.rem(v, 128) for v in own_maps])[0:1], 128)
    place, _ = places(dot(high, lows, NT))
    rank = jnp.zeros((1, 896), I32)
    for value, scale in ((place // 128, 128), (lax.rem(place, 128), 1)):
        found = dot(value.astype(F32).astype(BF16), lows) * high.astype(F32)
        rank = rank + jnp.sum(found, axis=0, keepdims=True).astype(I32) * scale
    select[...] = onehot(rank, 896)

    owners, slot_ids = [], []
    for k in range(4):
        owner = mapsb[pl.ds(pl.multiple_of((g * 16 + 4 * k + x) * 8, 8), 8), :] // 56
        hot = onehot(owner[0:1], 128)
        earlier = dot(hot, strict(224)) * hot.astype(F32)
        pos = jnp.sum(earlier, axis=0, keepdims=True).astype(I32)
        owners.append(owner)
        slot_ids.append(jnp.broadcast_to(pos + 3 * k, (8, 224)))
    owner, slot = joined(owners)[0:1], joined(slot_ids)[0:1]
    slots[0:1] = owner * 16 + slot

    factor(2)
    factor_pass(1)
    each(24, table, 16)
    for d in (0, 1):
        ref = srcb.at[pl.ds(2 * d, 2), x]
        wait(ref, vr.at[2, d])
    factor(3)
    factor_pass(2)
    sources = srcb[...].reshape(2048, 128)

    own_part = solved_own.at[:, pl.ds(pl.multiple_of(z * 128, 128), 128)]

    def solve(m):
        rows = invf[pl.ds(2 * m, 2)].reshape(256, 2048)
        solved_all[pl.ds(pl.multiple_of(m * 256, 256), 256), :] = dot(rows, sources).astype(BF16)

    each(8, solve)
    for i in (1, 2, 3):
        to = at(i, 0)
        remote(
            solved_all.at[pl.ds(pl.multiple_of(to * 128, 128), 128), :], own_part,
            cs.at[3, i], cr.at[3, i], to,
        ).start()
    own_s = pltpu.make_async_copy(
        solved_all.at[pl.ds(pl.multiple_of(h * 128, 128), 128), :], own_part, loc_sem.at[3]
    )
    own_s.start()
    la[z] = low[...]
    lb[x] = low[...]
    each(32, table, 24)
    starts_in = pltpu.make_async_copy(start, start_at, loc_sem.at[7])
    starts_in.start()

    every = mapsb[...]
    r = lax.broadcasted_iota(I32, (128, 1024), 0)
    c = lax.broadcasted_iota(I32, (128, 1024), 1)
    eighth = (c == 8 * r).astype(F32).astype(BF16)
    mine = (every // 56 == me).astype(F32)
    local = dot(eighth, ((lax.rem(every, 56) + 1).astype(F32) * mine).astype(BF16))
    mine = dot(eighth, mine.astype(BF16))
    pos = dot(mine.astype(BF16), strict(224))
    r = lax.broadcasted_iota(I32, (128, 64), 0)
    c = lax.broadcasted_iota(I32, (128, 64), 1)
    keep = lax.broadcasted_iota(I32, (8, 128), 1) // 16 == lax.broadcasted_iota(I32, (8, 128), 0)
    totals = [jnp.zeros((8, 64), F32) for _ in range(4)]
    for p in range(3):
        found = jnp.where(pos == p, local, 0.0).astype(BF16)
        line_of = dot(jnp.ones((8, 224), BF16), found, NT)
        line_of = jnp.where(keep, line_of, 0.0).astype(BF16)
        slot_of = 3 * lax.rem(r // 4, 4) + p
        for v in range(4):
            want = slot_of if v == 0 else slot_of - 4 * (v - 1) + 12
            fits = (lax.rem(r, 4) == c // 16) & (want == lax.rem(c, 16))
            if v > 0:
                fits = fits & (lax.rem(c, 16) >= 12)
            totals[v] = totals[v] + dot(line_of, fits.astype(F32).astype(BF16))
    for v in range(4):
        target[v] = totals[v].astype(I32) - 1

    factor_pass(3)
    for i in (1, 3):
        wait(held.at[z], cr.at[1, i])
    for d in (0, 1):
        wait(via.at[d], vr.at[1, d])
    own_sent.wait()
    for r in range(4):
        for a, (ref, mine, dz, dx) in enumerate(rings):
            for d, step in ((0, 1), (1, -1)):
                block = lax.rem(mine - step + 4, 4)
                wait(lpart(ref, block, 1 - d, r, -dz * step), lr.at[a, d, 1 - d, r])
                wait(lpart(ref, lax.rem(mine + 2, 4), d, r, 2 * dz), lr.at[a, 2, d, r])

    def rows_of(k):
        left = la[k]
        got = (held[k, :, 0:896].astype(F32) - dot(left, lb[...].reshape(896, 2048), NT)).astype(BF16)
        moved[k, :, 0:896] = dot(got, select[...], NT).astype(BF16)
        moved[k, :, 896:1024] = (held[k, :, 896:1024].astype(F32) - dot(left, solved_all[...])).astype(BF16)

    each(4, rows_of)

    def send_rows(j, first=0):
        grp = lax.rem(g + j, 8)
        row = lax.broadcasted_iota(I32, (256, 896), 0) + grp * 256
        main = (row == slots[0:1]).astype(F32).astype(BF16)
        def quarter(q):
            cols = moved[:, :, 256 * q : 256 * (q + 1)].reshape(896, 256)
            return dot(main, cols).reshape(16, 2, 8, 256)

        last = quarter(3)
        free = lax.broadcasted_iota(I32, (16, 8, 256), 1) >= 4
        turned = [jnp.concatenate([last[:, t, 4:], last[:, t, :4]], axis=1) for t in range(2)]
        for q, extra in enumerate((turned[0], last[:, 0], turned[1])):
            part = quarter(q)
            both = jnp.concatenate([part[:, 0], jnp.where(free, extra, part[:, 1])], axis=1)
            outs[pl.ds(grp * 16, 16), :, 256 * q : 256 * (q + 1)] = both.astype(BF16)

        def go(i):
            to = lax.rem(h + i, 16)

            pltpu.make_async_remote_copy(
                outs.at[grp * 16 + to], arrived.at[me], es, er.at[g], device_id=(grp, to), device_id_type=MESH
            ).start()

        each(16, go, first)

    send_rows(0, 1)
    own_rows = pltpu.make_async_copy(outs.at[me], arrived.at[me], er.at[g])
    own_rows.start()
    each(8, send_rows, 1)


    starts_in.wait()
    for copy in base:
        copy.wait()

    def spread(j):
        grp = lax.rem(g + 8 - j, 8)
        wait(arrived.at[pl.ds(grp * 16, 16)], er.at[grp])
        pick = [onehot_rows(target[v, pl.ds(grp, 1), :]) for v in range(4)]
        for b in range(4):
            got = arrived[pl.ds(grp * 16 + 4 * b, 4)].reshape(64, 768)
            tail = jnp.zeros((56, 256), F32)
            for q in range(3):
                part = dot(pick[0], got[:, 256 * q : 256 * (q + 1)])
                tile[b, 2 * q] = part[:, :128]
                tile[b, 2 * q + 1] = part[:, 128:]
                tail = tail + dot(pick[q + 1], got[:, 256 * q : 256 * (q + 1)])
            tile[b, 6] = tail[:, :128]
            tile[b, 7] = tail[:, 128:]
            right[:, 128 * b : 128 * (b + 1)] += tail[:, 128:]
        lane = lax.broadcasted_iota(I32, (56, 128), 1)

        def columns(s):
            for u in range(UNROLL):
                t = s * UNROLL + u
                cols = pl.ds(pl.multiple_of(t * 128, 128), 128)
                total = jnp.zeros((56, 128), F32)
                for b in range(4):
                    begin = start_at[grp * 4 + b, 0, t]
                    i = jnp.clip(begin // 128, 0, 6)
                    both = jnp.where(lane >= lax.rem(begin, 128), tile[b, i], tile[b, i + 1])
                    where = jnp.broadcast_to(index[grp * 4 + b, pl.ds(t, 1), :], (56, 128))
                    taken = jnp.take_along_axis(both, where & 127, axis=1)
                    total = jnp.where(where >= 0, taken, total)
                front[:, cols] += total

        each(56 // UNROLL, columns)

    each(8, spread)

    for d in (0, 1):
        for part in (0, 1):
            await_piece(h, part, zs.at[d, part])
            for r in range(4):
                await_piece(at(offsets[r], 0), part, xs.at[r, d, part])
        step = 2 * d - 1
        await_piece(at(step, 0), d, zs.at[2 + d, 0])
        for r in range(4):
            await_piece(at(offsets[r], step), d, xs.at[r, 2 + d, 0])
    for i in (1, 2, 3):
        wait(map_rows(me, 1), ms.at[0, i])
        wait(map_rows(line, 4), ms.at[1, i])
        wait(srcb.at[z, x], cs.at[0, i])
        if i != 2:
            wait(held.at[z], cs.at[1, i])
        if i != 2:
            wait(srcb.at[:, x], cs.at[2, i])
        wait(own_part, cs.at[3, i])
        wait(own_part, cr.at[3, i])
    for i in range(1, 8):
        wait(map_rows(0, 16), ms.at[2, i])
    for r in range(4):
        for a, (ref, mine_at, dz, dx) in enumerate(rings):
            for d in (0, 1):
                for part in (0, 1):
                    wait(lpart(ref, mine_at, part, r), ls.at[a, d, part, r])
                wait(lpart(ref, mine_at, d, r), ls.at[a, 2, d, r])
    for d in (0, 1):
        wait(via.at[d], vs.at[0, d])
        wait(via.at[d], vs.at[1, d])
        wait(srcb.at[pl.ds(2 * d, 2), x], vs.at[2, d])
    own_s.wait()
    wait(outs.at[pl.ds(0, 127)], es)


def main_call(inv, cross, contrib, csrc, psrc, emap, parent, rhs):
    dma = pltpu.SemaphoreType.DMA
    return pl.pallas_call(
        main_kernel,
        out_shape=(
            jax.ShapeDtypeStruct((56, 7168), F32),
            jax.ShapeDtypeStruct((56, 512), F32),
            jax.ShapeDtypeStruct((128, 512), BF16),
        ),
        in_specs=[hbm(), vmem(), hbm(), vmem(), vmem(), vmem(), hbm(), hbm()],
        out_specs=(vmem(), vmem(), hbm()),
        scratch_shapes=[
            pltpu.VMEM((16, 128, 2048), BF16),
            pltpu.VMEM((4, 4, 128, 128), BF16),
            pltpu.VMEM((224, 2048), BF16),
            pltpu.VMEM((4, 224, 2048), BF16),
            pltpu.VMEM((4, 224, 2048), BF16),
            pltpu.VMEM((224, 3584), F32),
            pltpu.VMEM((4, 224, 1024), BF16),
            pltpu.VMEM((4, 224, 1024), BF16),
            pltpu.VMEM((2048, 128), BF16),
            pltpu.VMEM((4, 224, 1024), BF16),
            pltpu.VMEM((896, 896), BF16),
            pltpu.VMEM((8, 896), I32),
            pltpu.VMEM((128, 16, 768), BF16),
            pltpu.VMEM((1024, 224), I32),
            pltpu.VMEM((128, 16, 768), BF16),
            pltpu.VMEM((32, 56, 128), I32),
            pltpu.VMEM((32, 8, 64), I32),
            pltpu.SMEM((32, 8, 64), I32),
            pltpu.VMEM((4, 8, 64), I32),
            pltpu.VMEM((4, 8, 56, 128), F32),
            pltpu.VMEM((2, 112, 1024), BF16),
            dma((3, 2)), dma((3, 2)),
            dma((8,)),
            dma((3, 8)), dma((3, 8)),
            dma((4, 2)), dma((4, 2)),
            dma((4, 4, 2)), dma((4, 4, 2)),
            dma((4, 4)), dma((4, 4)),
            dma((2, 3, 2, 4)), dma((2, 3, 2, 4)),
            dma, dma((8,)),
        ],
        compiler_params=pltpu.CompilerParams(
            collective_id=0, has_side_effects=True, vmem_limit_bytes=58 << 20
        ),
        name="fronts",
    )(inv, cross, contrib, csrc, psrc, emap, parent, rhs)


def on_device(
    pivot_inverse, cross_block, contrib_block, pivot_sources, contrib_sources, ext_map, parent_front, parent_rhs
):
    front, right, solved_own = main_call(
        pivot_inverse[0], cross_block[0], contrib_block[0], contrib_sources[0], pivot_sources[0],
        ext_map, parent_front, parent_rhs,
    )
    return solved_own[None], front, right


def solution(mesh):
    return jax.shard_map(
        on_device,
        mesh=mesh,
        in_specs=(
            P("grp", "hlp", None),
            P("grp", "hlp", None),
            P("grp", "hlp", None),
            P("grp", "hlp", None),
            P("grp", "hlp", None),
            P("grp", "hlp"),
            P(("grp", "hlp"), None),
            P(("grp", "hlp"), None),
        ),
        out_specs=(P("grp", "hlp", None), P(("grp", "hlp"), None), P(("grp", "hlp"), None)),
        check_vma=False,
    )
```

```python
import functools

import jax
import jax.numpy as jnp
from jax import lax
from jax.experimental import pallas as pl
from jax.experimental.pallas import tpu as pltpu
from jax.sharding import PartitionSpec as P

MESH = pl.DeviceIdType.MESH
F32, BF16, I32 = jnp.float32, jnp.bfloat16, jnp.int32
NT = (((1,), (1,)), ((), ()))
NN = (((1,), (0,)), ((), ()))
UNROLL = 14


def dot(a, b, dims=NN):
    return lax.dot_general(a, b, dims, preferred_element_type=F32)


def hbm():
    return pl.BlockSpec(memory_space=pl.ANY)


def vmem():
    return pl.BlockSpec(memory_space=pltpu.VMEM)


def onehot(ids, n):
    return (lax.broadcasted_iota(I32, (n, ids.shape[1]), 0) == ids).astype(F32).astype(BF16)


def onehot_rows(ids):
    return (lax.broadcasted_iota(I32, (56, ids.shape[1]), 0) == ids).astype(F32).astype(BF16)


def strict(n):
    r = lax.broadcasted_iota(I32, (n, n), 0)
    c = lax.broadcasted_iota(I32, (n, n), 1)
    return (r < c).astype(F32).astype(BF16)


def joined(parts):
    r = lax.broadcasted_iota(I32, (224, 896), 0)
    c = lax.broadcasted_iota(I32, (224, 896), 1)
    total = jnp.zeros((8, 896), F32)
    for b in range(4):
        shift = (c == r + 224 * b).astype(F32).astype(BF16)
        total = total + dot(parts[b].astype(F32).astype(BF16), shift)
    return total.astype(I32)


def places(member):
    mb = member.astype(BF16)
    before = dot(mb, strict(128))
    count = dot(mb, jnp.ones((128, 128), BF16)).astype(BF16)
    r = lax.broadcasted_iota(I32, (64, 64), 0)
    c = lax.broadcasted_iota(I32, (64, 64), 1)
    above = dot((c < r).astype(F32).astype(BF16), count)
    row_count = dot(jnp.ones((8, 128), BF16), mb, NT).astype(BF16)
    starts = dot(row_count, strict(64))
    return (before + above).astype(I32), starts.astype(I32)


def main_kernel(
    inv, cross, contrib, csrc, psrc, emap, parent, rhs,
    front, right, solved_own,
    invf, srcb, low, la, lb, cbuf, sent, held, solved_all, moved, select, slots, outs, mapsb,
    arrived, index, start, start_at, target, tile, via, vs, vr,
    loc_sem, ms, mr, zs, zr, xs, xr, cs, cr, ls, lr, es, er,
):
    g = lax.axis_index("grp")
    h = lax.axis_index("hlp")
    z, x = h // 4, lax.rem(h, 4)
    me = g * 16 + h

    def at(dz, dx):
        return lax.rem(z + dz + 4, 4) * 4 + lax.rem(x + dx + 4, 4)

    def chunks(block):
        return block // 2 + 1

    def each(count, fn, first=0):
        def body(c, carry):
            fn(c)
            return carry

        lax.fori_loop(first, count, body, 0)

    def remote(source, target, ssem, rsem, to):
        return pltpu.make_async_remote_copy(
            source, target, ssem, rsem, device_id={"hlp": to}, device_id_type=MESH
        )

    def wait(ref, sem):
        pltpu.make_async_copy(ref, ref, sem).wait()

    def who(grp, i):
        return lax.rem(grp + g, 8), lax.rem(h + i, 16)

    barrier = pltpu.get_barrier_semaphore()

    def greet(i):
        p = lax.rem(me + i, 128)
        pl.semaphore_signal(barrier, inc=1, device_id=(p // 16, lax.rem(p, 16)), device_id_type=MESH)

    each(128, greet, 1)
    own = pltpu.make_async_copy(inv, invf.at[h], loc_sem.at[0])
    load = pltpu.make_async_copy(contrib, cbuf, loc_sem.at[1])
    load.start()
    base = (
        pltpu.make_async_copy(parent, front, loc_sem.at[5]),
        pltpu.make_async_copy(rhs, right, loc_sem.at[6]),
    )
    for copy in base:
        copy.start()

    def clear(i):
        def chunk(c):
            invf[i, :, pl.ds(pl.multiple_of(c * 256, 256), 256)] = jnp.zeros((128, 256), BF16)

        each(8, chunk, chunks(i))

    each(16, clear)
    own.start()
    mapsb[pl.ds(pl.multiple_of(me * 8, 8), 8), :] = jnp.broadcast_to(emap[...], (8, 224))
    for b in range(4):
        @pl.when(z == b)
        def _():
            srcb[b, x] = psrc[:, 128 * b : 128 * (b + 1)]

    load.wait()
    for b in range(4):
        sent[b, :, 0:896] = cbuf[:, 896 * b : 896 * (b + 1)].astype(BF16)
        sent[b, :, 896:1024] = csrc[:, 128 * b : 128 * (b + 1)]
    own.wait()
    pl.semaphore_wait(barrier, 127)

    def sized(block, fn):
        for n in range(1, 9):
            pl.when(chunks(block) == n)(functools.partial(fn, 256 * n))

    def piece(block, n, part):
        return invf.at[block, pl.ds(64 * part, 64), pl.ds(0, n)]

    def map_rows(first, count):
        return mapsb.at[pl.ds(pl.multiple_of(first * 8, 8), count * 8), :]

    def send(block, part, ssem, rsem, to):
        def go(n):
            ref = piece(block, n, part)
            remote(ref, ref, ssem, rsem, to).start()

        sized(block, go)

    def await_piece(block, part, sem):
        sized(block, lambda n: wait(piece(block, n, part), sem))

    def send_both(block, ssem, rsem, right, left, parts):
        def go(n):
            for p in parts:
                for d, to in ((0, right), (1, left)):
                    part = p if d == 0 or len(parts) == 1 else 1 - p
                    ref = piece(block, n, part)
                    remote(ref, ref, ssem.at[d, part], rsem.at[d, part], to).start()

        sized(block, go)

    offsets = (0, -1, 1, 2)

    def send_x(r, parts=(0, 1)):
        send_both(at(offsets[r], 0), xs.at[r], xr.at[r], at(0, 1), at(0, -1), parts)

    def pass_x(r):
        for d, dx in ((0, -1), (1, 1)):
            block = at(offsets[r], dx)

            def go(n, d=d, dx=dx, block=block):
                ref = piece(block, n, d)
                wait(ref, xr.at[r, d, d])
                remote(ref, ref, xs.at[r, 2 + d, 0], xr.at[r, 2 + d, 0], at(0, -dx)).start()

            sized(block, go)

    for i in (1, 2, 3):
        remote(map_rows(me, 1), map_rows(me, 1), ms.at[0, i], mr.at[0, i], at(0, i)).start()
    send_both(h, zs, zr, at(1, 0), at(-1, 0), (0, 1))
    send_x(0)
    for i in (1, 2, 3):
        to = lax.rem(z + i, 4)
        cols = pl.ds(pl.multiple_of(to * 128, 128), 128)
        remote(psrc.at[:, cols], srcb.at[z, x], cs.at[0, i], cr.at[0, i], at(i, 0)).start()
    for i in (1, 2, 3):
        wait(map_rows(me, 1), mr.at[0, i])
    line = g * 16 + z * 4
    for i in (1, 2, 3):
        remote(map_rows(line, 4), map_rows(line, 4), ms.at[1, i], mr.at[1, i], at(i, 0)).start()

    for d, dz in ((0, -1), (1, 1)):
        block = at(dz, 0)
        await_piece(block, d, zr.at[d, d])
        send(block, d, zs.at[2 + d, 0], zr.at[2 + d, 0], at(-dz, 0))
        send_x(1 + d, (d,))
    for d, dz in ((0, -1), (1, 1)):
        await_piece(at(dz, 0), 1 - d, zr.at[d, 1 - d])
        send_x(1 + d, (1 - d,))
    for d, i in ((0, 1), (1, 3)):
        part = pl.ds(112 * d, 112)
        remote(sent.at[lax.rem(z + 2, 4), part, :], via.at[d], vs.at[0, d], vr.at[0, d], at(i, 0)).start()
    for i in (1, 3):
        remote(sent.at[lax.rem(z + i, 4)], held.at[z], cs.at[1, i], cr.at[1, i], at(i, 0)).start()
    own_sent = pltpu.make_async_copy(sent.at[z], held.at[z], loc_sem.at[2])
    own_sent.start()
    for i in (1, 2, 3):
        wait(map_rows(line, 4), mr.at[1, i])
    for i in range(1, 8):
        pltpu.make_async_remote_copy(
            map_rows(g * 16, 16), map_rows(g * 16, 16), ms.at[2, i], mr.at[2, i],
            device_id=(lax.rem(g + i, 8), h), device_id_type=MESH,
        ).start()
    pass_x(0)
    for i in (1, 2, 3):
        wait(srcb.at[z, x], cr.at[0, i])
    for i in (1, 3):
        remote(srcb.at[:, x], srcb.at[:, x], cs.at[2, i], cr.at[2, i], at(0, i)).start()

    for d in (0, 1):
        await_piece(at(2, 0), d, zr.at[2 + d, 0])
        send_x(3, (d,))
    pass_x(1)

    rings = ((la, z, 1, 0), (lb, x, 0, 1))

    def slab(r, dz=0):
        return pl.ds(pl.multiple_of(lax.rem(z + dz + offsets[r] + 4, 4) * 512, 512), 512)

    def lpart(ref, i, part, r, dz=0):
        return ref.at[i, pl.ds(112 * part, 112), slab(r, dz)]

    def factor(r):
        block = at(offsets[r], 2)

        await_piece(at(offsets[r], -1), 1, xr.at[r, 0, 1])
        await_piece(at(offsets[r], 1), 0, xr.at[r, 1, 0])
        await_piece(block, 0, xr.at[r, 2, 0])
        await_piece(block, 1, xr.at[r, 3, 0])
        zz = lax.rem(z + offsets[r] + 4, 4)
        for part in range(2):
            m = 2 * zz + part
            rows = invf[pl.ds(2 * m, 2)].reshape(256, 2048)
            low[:, pl.ds(pl.multiple_of(m * 256, 256), 256)] = dot(cross[...], rows, NT).astype(BF16)
        for order in (0, 1):
            for a, (ref, mine, dz, dx) in enumerate(rings):
                for d, step in ((0, 1), (1, -1)):
                    part = order if d == 0 else 1 - order
                    remote(
                        low.at[pl.ds(112 * part, 112), slab(r)], lpart(ref, mine, part, r),
                        ls.at[a, d, part, r], lr.at[a, d, part, r], at(dz * step, dx * step),
                    ).start()

    def factor_pass(r):
        for a, (ref, mine, dz, dx) in enumerate(rings):
            for d, step in ((0, 1), (1, -1)):
                block = lax.rem(mine - step + 4, 4)
                part = lpart(ref, block, d, r, -dz * step)
                wait(part, lr.at[a, d, d, r])
                remote(part, part, ls.at[a, 2, d, r], lr.at[a, 2, d, r], at(dz * step, dx * step)).start()

    def table(i):
        member = jnp.zeros((64, 128), F32)
        for b in range(4):
            v = mapsb[pl.ds(pl.multiple_of((4 * i + b) * 8, 8), 8), :][0:1]
            member = member + dot(onehot(v // 128, 64), onehot(lax.rem(v, 128), 128), NT)
        place, starts = places(member)
        index[i] = jnp.where(member > 0.5, lax.rem(place, 128), -1)[:56]
        start[i] = jnp.clip(starts, 0, 895)

    for d, i in ((0, 1), (1, 3)):
        wait(via.at[d], vr.at[0, d])
        origin = lax.rem(z + 4 - i, 4)
        remote(
            via.at[d], held.at[origin, pl.ds(112 * d, 112), :], vs.at[1, d], vr.at[1, d], at(i, 0)
        ).start()
    factor(0)
    for i in range(1, 8):
        wait(map_rows(0, 16), mr.at[2, i])
    pass_x(2)
    for d, i in ((0, 1), (1, 3)):
        wait(srcb.at[:, x], cr.at[2, i])
        ref = srcb.at[pl.ds(2 * d, 2), lax.rem(x + 4 - i, 4)]
        remote(ref, ref, vs.at[2, d], vr.at[2, d], at(0, i)).start()
    factor(1)
    factor_pass(0)
    each(8, table)
    pass_x(3)

    own_maps = [mapsb[pl.ds(pl.multiple_of((line + b) * 8, 8), 8), :] for b in range(4)]
    high = onehot(joined([v // 128 for v in own_maps])[0:1], 64)
    lows = onehot(joined([lax.rem(v, 128) for v in own_maps])[0:1], 128)
    place, _ = places(dot(high, lows, NT))
    rank = jnp.zeros((1, 896), I32)
    for value, scale in ((place // 128, 128), (lax.rem(place, 128), 1)):
        found = dot(value.astype(F32).astype(BF16), lows) * high.astype(F32)
        rank = rank + jnp.sum(found, axis=0, keepdims=True).astype(I32) * scale
    select[...] = onehot(rank, 896)

    owners, slot_ids = [], []
    for k in range(4):
        owner = mapsb[pl.ds(pl.multiple_of((g * 16 + 4 * k + x) * 8, 8), 8), :] // 56
        hot = onehot(owner[0:1], 128)
        earlier = dot(hot, strict(224)) * hot.astype(F32)
        pos = jnp.sum(earlier, axis=0, keepdims=True).astype(I32)
        owners.append(owner)
        slot_ids.append(jnp.broadcast_to(pos + 3 * k, (8, 224)))
    owner, slot = joined(owners)[0:1], joined(slot_ids)[0:1]
    slots[0:1] = owner * 16 + slot

    factor(2)
    factor_pass(1)
    each(16, table, 8)
    for d in (0, 1):
        ref = srcb.at[pl.ds(2 * d, 2), x]
        wait(ref, vr.at[2, d])
    factor(3)
    factor_pass(2)
    sources = srcb[...].reshape(2048, 128)

    own_part = solved_own.at[:, pl.ds(pl.multiple_of(z * 128, 128), 128)]

    def solve(m):
        rows = invf[pl.ds(2 * m, 2)].reshape(256, 2048)
        solved_all[pl.ds(pl.multiple_of(m * 256, 256), 256), :] = dot(rows, sources).astype(BF16)

    each(8, solve)
    for i in (1, 2, 3):
        to = at(i, 0)
        remote(
            solved_all.at[pl.ds(pl.multiple_of(to * 128, 128), 128), :], own_part,
            cs.at[3, i], cr.at[3, i], to,
        ).start()
    own_s = pltpu.make_async_copy(
        solved_all.at[pl.ds(pl.multiple_of(h * 128, 128), 128), :], own_part, loc_sem.at[3]
    )
    own_s.start()
    la[z] = low[...]
    lb[x] = low[...]
    each(32, table, 16)
    starts_in = pltpu.make_async_copy(start, start_at, loc_sem.at[7])
    starts_in.start()

    every = mapsb[...]
    r = lax.broadcasted_iota(I32, (128, 1024), 0)
    c = lax.broadcasted_iota(I32, (128, 1024), 1)
    eighth = (c == 8 * r).astype(F32).astype(BF16)
    mine = (every // 56 == me).astype(F32)
    local = dot(eighth, ((lax.rem(every, 56) + 1).astype(F32) * mine).astype(BF16))
    mine = dot(eighth, mine.astype(BF16))
    pos = dot(mine.astype(BF16), strict(224))
    r = lax.broadcasted_iota(I32, (128, 64), 0)
    c = lax.broadcasted_iota(I32, (128, 64), 1)
    keep = lax.broadcasted_iota(I32, (8, 128), 1) // 16 == lax.broadcasted_iota(I32, (8, 128), 0)
    totals = [jnp.zeros((8, 64), F32) for _ in range(4)]
    for p in range(3):
        found = jnp.where(pos == p, local, 0.0).astype(BF16)
        line_of = dot(jnp.ones((8, 224), BF16), found, NT)
        line_of = jnp.where(keep, line_of, 0.0).astype(BF16)
        slot_of = 3 * lax.rem(r // 4, 4) + p
        for v in range(4):
            want = slot_of if v == 0 else slot_of - 4 * (v - 1) + 12
            fits = (lax.rem(r, 4) == c // 16) & (want == lax.rem(c, 16))
            if v > 0:
                fits = fits & (lax.rem(c, 16) >= 12)
            totals[v] = totals[v] + dot(line_of, fits.astype(F32).astype(BF16))
    for v in range(4):
        target[v] = totals[v].astype(I32) - 1

    factor_pass(3)
    for i in (1, 3):
        wait(held.at[z], cr.at[1, i])
    for d in (0, 1):
        wait(via.at[d], vr.at[1, d])
    own_sent.wait()
    for r in range(4):
        for a, (ref, mine, dz, dx) in enumerate(rings):
            for d, step in ((0, 1), (1, -1)):
                block = lax.rem(mine - step + 4, 4)
                wait(lpart(ref, block, 1 - d, r, -dz * step), lr.at[a, d, 1 - d, r])
                wait(lpart(ref, lax.rem(mine + 2, 4), d, r, 2 * dz), lr.at[a, 2, d, r])

    def rows_of(k):
        left = la[k]
        got = (held[k, :, 0:896].astype(F32) - dot(left, lb[...].reshape(896, 2048), NT)).astype(BF16)
        moved[k, :, 0:896] = dot(got, select[...], NT).astype(BF16)
        moved[k, :, 896:1024] = (held[k, :, 896:1024].astype(F32) - dot(left, solved_all[...])).astype(BF16)

    each(4, rows_of)

    def send_rows(j, first=0):
        grp = lax.rem(g + j, 8)
        row = lax.broadcasted_iota(I32, (256, 896), 0) + grp * 256
        main = (row == slots[0:1]).astype(F32).astype(BF16)
        def quarter(q):
            cols = moved[:, :, 256 * q : 256 * (q + 1)].reshape(896, 256)
            return dot(main, cols).reshape(16, 2, 8, 256)

        last = quarter(3)
        free = lax.broadcasted_iota(I32, (16, 8, 256), 1) >= 4
        turned = [jnp.concatenate([last[:, t, 4:], last[:, t, :4]], axis=1) for t in range(2)]
        for q, extra in enumerate((turned[0], last[:, 0], turned[1])):
            part = quarter(q)
            both = jnp.concatenate([part[:, 0], jnp.where(free, extra, part[:, 1])], axis=1)
            outs[pl.ds(grp * 16, 16), :, 256 * q : 256 * (q + 1)] = both.astype(BF16)

        def go(i):
            to = lax.rem(h + i, 16)

            pltpu.make_async_remote_copy(
                outs.at[grp * 16 + to], arrived.at[me], es, er.at[g], device_id=(grp, to), device_id_type=MESH
            ).start()

        each(16, go, first)

    send_rows(0, 1)
    own_rows = pltpu.make_async_copy(outs.at[me], arrived.at[me], er.at[g])
    own_rows.start()
    each(8, send_rows, 1)


    starts_in.wait()
    for copy in base:
        copy.wait()

    def spread(j):
        grp = lax.rem(g + 8 - j, 8)
        wait(arrived.at[pl.ds(grp * 16, 16)], er.at[grp])
        pick = [onehot_rows(target[v, pl.ds(grp, 1), :]) for v in range(4)]
        for b in range(4):
            got = arrived[pl.ds(grp * 16 + 4 * b, 4)].reshape(64, 768)
            tail = jnp.zeros((56, 256), F32)
            for q in range(3):
                part = dot(pick[0], got[:, 256 * q : 256 * (q + 1)])
                tile[b, 2 * q] = part[:, :128]
                tile[b, 2 * q + 1] = part[:, 128:]
                tail = tail + dot(pick[q + 1], got[:, 256 * q : 256 * (q + 1)])
            tile[b, 6] = tail[:, :128]
            tile[b, 7] = tail[:, 128:]
            right[:, 128 * b : 128 * (b + 1)] += tail[:, 128:]
        lane = lax.broadcasted_iota(I32, (56, 128), 1)

        def columns(s):
            for u in range(UNROLL):
                t = s * UNROLL + u
                cols = pl.ds(pl.multiple_of(t * 128, 128), 128)
                total = jnp.zeros((56, 128), F32)
                for b in range(4):
                    begin = start_at[grp * 4 + b, 0, t]
                    i = jnp.clip(begin // 128, 0, 6)
                    both = jnp.where(lane >= lax.rem(begin, 128), tile[b, i], tile[b, i + 1])
                    where = jnp.broadcast_to(index[grp * 4 + b, pl.ds(t, 1), :], (56, 128))
                    taken = jnp.take_along_axis(both, where & 127, axis=1)
                    total = jnp.where(where >= 0, taken, total)
                front[:, cols] += total

        each(56 // UNROLL, columns)

    each(8, spread)

    for d in (0, 1):
        for part in (0, 1):
            await_piece(h, part, zs.at[d, part])
            for r in range(4):
                await_piece(at(offsets[r], 0), part, xs.at[r, d, part])
        step = 2 * d - 1
        await_piece(at(step, 0), d, zs.at[2 + d, 0])
        for r in range(4):
            await_piece(at(offsets[r], step), d, xs.at[r, 2 + d, 0])
    for i in (1, 2, 3):
        wait(map_rows(me, 1), ms.at[0, i])
        wait(map_rows(line, 4), ms.at[1, i])
        wait(srcb.at[z, x], cs.at[0, i])
        if i != 2:
            wait(held.at[z], cs.at[1, i])
        if i != 2:
            wait(srcb.at[:, x], cs.at[2, i])
        wait(own_part, cs.at[3, i])
        wait(own_part, cr.at[3, i])
    for i in range(1, 8):
        wait(map_rows(0, 16), ms.at[2, i])
    for r in range(4):
        for a, (ref, mine_at, dz, dx) in enumerate(rings):
            for d in (0, 1):
                for part in (0, 1):
                    wait(lpart(ref, mine_at, part, r), ls.at[a, d, part, r])
                wait(lpart(ref, mine_at, d, r), ls.at[a, 2, d, r])
    for d in (0, 1):
        wait(via.at[d], vs.at[0, d])
        wait(via.at[d], vs.at[1, d])
        wait(srcb.at[pl.ds(2 * d, 2), x], vs.at[2, d])
    own_s.wait()
    wait(outs.at[pl.ds(0, 127)], es)


def main_call(inv, cross, contrib, csrc, psrc, emap, parent, rhs):
    dma = pltpu.SemaphoreType.DMA
    return pl.pallas_call(
        main_kernel,
        out_shape=(
            jax.ShapeDtypeStruct((56, 7168), F32),
            jax.ShapeDtypeStruct((56, 512), F32),
            jax.ShapeDtypeStruct((128, 512), BF16),
        ),
        in_specs=[hbm(), vmem(), hbm(), vmem(), vmem(), vmem(), hbm(), hbm()],
        out_specs=(vmem(), vmem(), hbm()),
        scratch_shapes=[
            pltpu.VMEM((16, 128, 2048), BF16),
            pltpu.VMEM((4, 4, 128, 128), BF16),
            pltpu.VMEM((224, 2048), BF16),
            pltpu.VMEM((4, 224, 2048), BF16),
            pltpu.VMEM((4, 224, 2048), BF16),
            pltpu.VMEM((224, 3584), F32),
            pltpu.VMEM((4, 224, 1024), BF16),
            pltpu.VMEM((4, 224, 1024), BF16),
            pltpu.VMEM((2048, 128), BF16),
            pltpu.VMEM((4, 224, 1024), BF16),
            pltpu.VMEM((896, 896), BF16),
            pltpu.VMEM((8, 896), I32),
            pltpu.VMEM((128, 16, 768), BF16),
            pltpu.VMEM((1024, 224), I32),
            pltpu.VMEM((128, 16, 768), BF16),
            pltpu.VMEM((32, 56, 128), I32),
            pltpu.VMEM((32, 8, 64), I32),
            pltpu.SMEM((32, 8, 64), I32),
            pltpu.VMEM((4, 8, 64), I32),
            pltpu.VMEM((4, 8, 56, 128), F32),
            pltpu.VMEM((2, 112, 1024), BF16),
            dma((3, 2)), dma((3, 2)),
            dma((8,)),
            dma((3, 8)), dma((3, 8)),
            dma((4, 2)), dma((4, 2)),
            dma((4, 4, 2)), dma((4, 4, 2)),
            dma((4, 4)), dma((4, 4)),
            dma((2, 3, 2, 4)), dma((2, 3, 2, 4)),
            dma, dma((8,)),
        ],
        compiler_params=pltpu.CompilerParams(
            collective_id=0, has_side_effects=True, vmem_limit_bytes=58 << 20
        ),
        name="fronts",
    )(inv, cross, contrib, csrc, psrc, emap, parent, rhs)


def on_device(
    pivot_inverse, cross_block, contrib_block, pivot_sources, contrib_sources, ext_map, parent_front, parent_rhs
):
    front, right, solved_own = main_call(
        pivot_inverse[0], cross_block[0], contrib_block[0], contrib_sources[0], pivot_sources[0],
        ext_map, parent_front, parent_rhs,
    )
    return solved_own[None], front, right


def solution(mesh):
    return jax.shard_map(
        on_device,
        mesh=mesh,
        in_specs=(
            P("grp", "hlp", None),
            P("grp", "hlp", None),
            P("grp", "hlp", None),
            P("grp", "hlp", None),
            P("grp", "hlp", None),
            P("grp", "hlp"),
            P(("grp", "hlp"), None),
            P(("grp", "hlp"), None),
        ),
        out_specs=(P("grp", "hlp", None), P(("grp", "hlp"), None), P(("grp", "hlp"), None)),
        check_vma=False,
    )
```
